256 devices in a mesh: roll: 32 (over y_lo, z, core), trans: 8 (over y_hi, x).
Axes of the slice: x: 4, y: 4 (y_hi: 2, y_lo: 2; y = y_hi * 2 + y_lo), z: 8, core: 2. Of those that a mesh axis runs over, the one named last changes fastest.
Arguments:
- adjoint: float32 [4, 2, 32, 256, 1024], P(None, None, None, 'roll', 'trans'), may hold values from -6 to 6
- source: float32 [4, 2, 32, 256, 1024], P(None, None, None, 'roll', 'trans'), may hold values from -6 to 6
- pressure: float32 [2, 256, 1024], P(None, 'roll', 'trans'), may hold values from -4 to 4
- film: float32 [256, 1024], P('roll', 'trans'), may hold values from 0.6 to 1.4
- cavity: int32 [2, 256, 1024], P(None, 'roll', 'trans'), may hold values 0 or 1
- temp_index: int32 [2], replicated, may hold values from 0 to 7
Outputs:
- adjoint_out: float32 [4, 2, 32, 256, 1024], P(None, None, None, 'roll', 'trans')
- wall_step: float32 [256, 1024], P('roll', 'trans')
The draws below stay inside these ranges and needn't reach their ends.
All inputs are finite; a program needn't handle non-finite values. No bound on the sum of `cavity` on one device may be relied on, other than what follows from the above.
Results may differ from the reference program's by a relative error of at most 0.00002.
Values sent between devices are 32-bit elements; how exact they have to be, the bound alone decides.
A program may use at most 64 MiB of HBM per device.

```python
import jax
import jax.numpy as jnp
from jax import lax

NZ = 32
CASES = 2
SECTIONS = 2
NX = 256
NY = 1024


def touch_ends(values, stream_key, low, largest):
    longest = values.shape.index(max(values.shape))
    spots = []
    for shift in (0, 1):
        where = [jax.random.randint(jax.random.fold_in(stream_key, axis), (), 0, length) for axis, length in enumerate(values.shape)]
        where[longest] = (where[longest] + shift) % values.shape[longest]
        spots.append(tuple(where))
    return values.at[spots[0]].set(low).at[spots[1]].set(largest)


def levels(own_key, extent, split, smallest, largest):
    gain = 1.0
    for position, parts in split:
        draws = jax.random.uniform(jax.random.fold_in(jax.random.fold_in(own_key, 6), position), (parts,), jnp.float32, smallest / len(split), largest / len(split))
        gain = gain * jnp.repeat(jnp.exp(draws), extent[position] // parts).reshape((-1,) + (1,) * (len(extent) - 1 - position))
    return gain


def gaussian(own_key, extent, width, most, shards=(), held_as=jnp.bfloat16):
    array = width * jax.random.normal(own_key, extent, jnp.float32)
    if shards:
        array = array * levels(own_key, extent, shards, -0.22, 0.18)
    return jnp.clip(array, -most, most).astype(held_as)


def setup_inputs(seed: int = 0) -> dict:
    key_of = jax.random.split(jax.random.key(seed), 7)
    return {
        "adjoint": gaussian(key_of[0], (4, CASES, NZ, NX, NY), 1.0, 6.0, ((3, 32), (4, 8)), jnp.float32),
        "source": gaussian(key_of[1], (4, CASES, NZ, NX, NY), 1.0, 6.0, ((3, 32), (4, 8)), jnp.float32),
        "pressure": gaussian(key_of[2], (CASES, NX, NY), 1.0, 4.0, ((1, 32), (2, 8)), jnp.float32),
        "film": jnp.clip(0.6 + 0.79999995 * jax.random.uniform(key_of[3], (NX, NY), jnp.float32) ** levels(key_of[3], (NX, NY), ((0, 32), (1, 8)), -0.2, 0.2), 0.6, 1.4),
        "cavity": touch_ends((jax.random.randint(key_of[4], (CASES, NX, NY), 0, 3) < 1).astype(jnp.int32), jax.random.fold_in(key_of[4], 1), 0, 1),
        "temp_index": jax.random.randint(key_of[5], (CASES,), 0, 8).astype(jnp.int32),
    }


VISCOSITY_PRESS = 0.3
VISCOSITY_TEMP = 0.5
THETA_STEP = 0.2
SOUND = 0.5
KAPPA = 0.6
HEATING = 0.3
ROLL_SPEED = 1.0
COURANT = 0.8

def coefficients(pressure, film, cavity, temp_index):
    implicit_weight = THETA_STEP * temp_index.astype(jnp.float32)
    fluid_viscosity = jnp.exp(VISCOSITY_PRESS * pressure - VISCOSITY_TEMP * implicit_weight[:, None, None])
    film_coef = 4.0 * fluid_viscosity / (film * film)
    density = 1.0 - 0.6 * cavity.astype(jnp.float32)
    pseudo_step = COURANT / (32.0 / 3.0 * fluid_viscosity + 4.0 * film_coef + 2.0 * SOUND + 1.0)
    return jnp.stack([fluid_viscosity, film_coef, density, pseudo_step])

def time_section(padded, source, coeffs):
    depth = source.shape[-3]
    width_x = source.shape[-2]
    width_y = source.shape[-1]

    def along_x(offset):
        return padded[..., 2 + offset:2 + offset + width_x, 2:2 + width_y]

    def along_y(offset):
        return padded[..., 2:2 + width_x, 2 + offset:2 + offset + width_y]
    center = along_x(0)
    second_x = (-along_x(2) + 16.0 * along_x(1) - 30.0 * center + 16.0 * along_x(-1) - along_x(-2)) / 12.0
    second_y = (-along_y(2) + 16.0 * along_y(1) - 30.0 * center + 16.0 * along_y(-1) - along_y(-2)) / 12.0
    first_x = (-along_x(2) + 8.0 * along_x(1) - 8.0 * along_x(-1) + along_x(-2)) / 12.0
    first_y = (-along_y(2) + 8.0 * along_y(1) - 8.0 * along_y(-1) + along_y(-2)) / 12.0
    layered = jnp.pad(center, ((0, 0), (0, 0), (1, 1), (0, 0), (0, 0)))
    second_z = layered[:, :, 2:] - 2.0 * center + layered[:, :, :-2]
    fluid_viscosity = coeffs[0][:, None]
    film_coef = coeffs[1][:, None]
    density = coeffs[2][:, None]
    pseudo_step = coeffs[3][:, None]
    film_height = ((jnp.arange(depth).astype(jnp.float32) + 0.5) / depth)[:, None, None]
    diffused = fluid_viscosity * (second_x + second_y) + film_coef * second_z
    carried = density * ROLL_SPEED * film_height * first_x
    resid_density = 0.5 * diffused[0] + carried[0] + SOUND * (first_x[1] + first_y[2])
    resid_along = diffused[1] + carried[1] + SOUND * first_x[0]
    resid_across = diffused[2] + carried[2] + SOUND * first_y[0]
    resid_energy = KAPPA * diffused[3] + carried[3] + HEATING * fluid_viscosity * center[1]
    residual = jnp.stack([resid_density, resid_along, resid_across, resid_energy])
    return center + pseudo_step * (residual + source)

def wall_terms(padded_mean, momentum, coeffs, film):
    width_x = momentum.shape[-2]
    depth = momentum.shape[-3]
    slope = (-padded_mean[:, 4:4 + width_x] + 8.0 * padded_mean[:, 3:3 + width_x] - 8.0 * padded_mean[:, 1:1 + width_x] + padded_mean[:, 0:width_x]) / 12.0
    layered = jnp.pad(momentum, ((0, 0), (1, 1), (0, 0), (0, 0)))
    bending = layered[:, 2:] - 2.0 * momentum + layered[:, :-2]
    curvature = lax.optimization_barrier(jnp.sum(momentum * bending, axis=1)) / depth
    flux = coeffs[2] * ROLL_SPEED * film / 2.0
    return flux * slope - 8.0 * coeffs[0] / (film * film * film) * curvature

def reference(adjoint, source, pressure, film, cavity, temp_index):

    def one_case(model_inputs):
        state_case, source_case, pressure_case, cavity_case, level_case = model_inputs
        state = state_case[:, None]
        forcing = source_case[:, None]
        coeffs = coefficients(pressure_case[None], film, cavity_case[None], level_case[None])
        for section_index in range(SECTIONS):
            padded = jnp.pad(state, ((0, 0), (0, 0), (0, 0), (2, 2), (2, 2)))
            state = time_section(padded, forcing, coeffs)
        depth = state.shape[2]
        mean_density = lax.optimization_barrier(jnp.sum(state[0], axis=1)) / depth
        padded_mean = jnp.pad(mean_density, ((0, 0), (2, 2), (0, 0)))
        terms = wall_terms(padded_mean, state[1], coeffs, film)
        return (state[:, 0], terms[0])
    states, terms = lax.map(one_case, (jnp.moveaxis(adjoint, 1, 0), jnp.moveaxis(source, 1, 0), pressure, cavity, temp_index))
    adjoint_out = jnp.moveaxis(states, 0, 1)
    wall_grad = lax.optimization_barrier(jnp.sum(terms, axis=0))
    total = jnp.sum(wall_grad * wall_grad)
    wall_step = wall_grad / jnp.sqrt(total / (NX * NY) + 1e-06)
    return (adjoint_out, wall_step)
```

```python
import jax
import jax.numpy as jnp
from jax import lax
from jax.experimental import pallas as pl
from jax.experimental.pallas import tpu as pltpu
from jax.sharding import PartitionSpec as P

VISCOSITY_PRESS = 0.3
VISCOSITY_TEMP = 0.5
THETA_STEP = 0.2
SOUND = 0.5
KAPPA = 0.6
HEATING = 0.3
COURANT = 0.8

MESH = pl.DeviceIdType.MESH
NC = 4
CASES = 2
NZ = 32
NX = 8
NY = 128
Z0 = 8
ZROWS = 48
ZT = NZ // 8
ZRING = 8
GROUPS = ((0, 3), (3, 1))

STEP, SLOPE, COUPLE, HEAT, A0, A1, A3, B0, B1, B3, C0, C1, C3 = range(13)
AROW = (A0, A1, A1, A3)
BROW = (B0, B1, B1, B3)
CROW = (C0, C1, C1, C3)


def kernel(
    adjoint, source, pressure, film, cavity, temp, out, wall,
    s0, s1, fin, src, coef, ysend, yleft, yright, mean, curv, mine, plane, mine2, ring,
    in_sem, src_sem, out_sem, xsend_sem, xrecv_sem, ysend_sem, yrecv_sem,
    msend_sem, mrecv_sem, rsend_sem, rrecv_sem,
):
    nr, nt = lax.axis_size("roll"), lax.axis_size("trans")
    r, t = lax.axis_index("roll"), lax.axis_index("trans")
    core = lax.rem(r, 2)
    z = lax.rem(r // 2, ZRING)
    g = r // (2 * ZRING)
    groups = nr // (2 * ZRING)
    plane_n = groups * 2 * nt
    cells = nr * NX * nt * NY

    def plane_peer(o):
        dt, dg, dc = o // (2 * groups), (o // 2) % groups, o % 2
        row = (lax.rem(g + dg, groups) * ZRING + z) * 2 + lax.rem(core + dc, 2)
        return (row, lax.rem(t + dt, nt))

    def ring_peer(o):
        return ((g * ZRING + lax.rem(z + o, ZRING)) * 2 + core, t)

    up = (lax.rem(r + 1, nr), t)
    down = (lax.rem(r + nr - 1, nr), t)
    right = (r, lax.rem(t + 1, nt))
    left = (r, lax.rem(t + nt - 1, nt))
    has_up, has_down = r < nr - 1, r > 0
    has_right, has_left = t < nt - 1, t > 0

    loads, src_loads = [], []
    for case in range(CASES):
        for x in range(NX):
            loads.append(pltpu.make_async_copy(
                adjoint.at[:, case, :, x, :], s0.at[case, :, 2 + x, Z0:Z0 + NZ, :], in_sem.at[case, x]))
            src_loads.append(pltpu.make_async_copy(
                source.at[:, case, :, x, :], src.at[case, :, x], src_sem.at[case, x]))
    for copy in loads:
        copy.start()
    for copy in src_loads:
        copy.start()

    barrier = pltpu.get_barrier_semaphore()
    for o in range(1, plane_n):
        pl.semaphore_signal(barrier, inc=1, device_id=plane_peer(o), device_id_type=MESH)
    for o in range(1, ZRING):
        pl.semaphore_signal(barrier, inc=1, device_id=ring_peer(o), device_id_type=MESH)
    for peer in (up, down):
        pl.semaphore_signal(barrier, inc=1, device_id=peer, device_id_type=MESH)

    thick = film[...]
    for case in range(CASES):
        theta = THETA_STEP * temp[case].astype(jnp.float32)
        visc = jnp.exp(VISCOSITY_PRESS * pressure[case] - VISCOSITY_TEMP * theta)
        fcoef = 4.0 * visc / (thick * thick)
        density = 1.0 - 0.6 * cavity[case].astype(jnp.float32)
        step = COURANT / (32.0 / 3.0 * visc + 4.0 * fcoef + 2.0 * SOUND + 1.0)
        sv, sf = step * visc, step * fcoef
        rows = {
            STEP: step, SLOPE: step * density / 12.0, COUPLE: step * (SOUND / 12.0), HEAT: HEATING * sv,
        }
        for scale, a, b, c in ((0.5, A0, B0, C0), (1.0, A1, B1, C1), (KAPPA, A3, B3, C3)):
            rows[a] = (scale / 12.0) * sv
            rows[b] = scale * sf
            rows[c] = 1.0 - scale * (5.0 * sv + 2.0 * sf)
        for k, value in rows.items():
            coef[case, k] = value

    zero8 = jnp.zeros((8, NY), jnp.float32)
    for buf in (s0, s1):
        for case in range(CASES):
            def clear(i, _, buf=buf, case=case):
                for c in range(NC):
                    buf[case, c, i, 0:Z0, :] = zero8
                    buf[case, c, i, Z0 + NZ:ZROWS, :] = zero8
                return 0
            lax.fori_loop(0, NX + 4, clear, 0)
    for case in range(CASES):
        def clear(i, _, case=case):
            fin[case, i, 0:Z0, :] = zero8
            fin[case, i, Z0 + NZ:ZROWS, :] = zero8
            return 0
        lax.fori_loop(0, NX, clear, 0)

    def clear_slab(first):
        for buf in (s0, s1):
            for case in range(CASES):
                for c in range(NC):
                    for x in (first, first + 1):
                        buf[case, c, x, Z0:Z0 + NZ, :] = jnp.zeros((NZ, NY), jnp.float32)

    @pl.when(jnp.logical_not(has_down))
    def _():
        clear_slab(0)
        mean[0:2] = jnp.zeros((2, CASES, NY), jnp.float32)

    @pl.when(jnp.logical_not(has_up))
    def _():
        clear_slab(NX + 2)
        mean[NX + 2:NX + 4] = jnp.zeros((2, CASES, NY), jnp.float32)

    @pl.when(jnp.logical_not(has_left))
    def _():
        yleft[...] = jnp.zeros(yleft.shape, jnp.float32)

    @pl.when(jnp.logical_not(has_right))
    def _():
        yright[...] = jnp.zeros(yright.shape, jnp.float32)

    lane = lax.broadcasted_iota(jnp.int32, (8, NY), 1)
    sub = lax.broadcasted_iota(jnp.int32, (8, NY), 0)
    lane4 = lane // 4
    lo_half = lane % 4 < 2
    first1, first2, last1, last2 = lane == 0, lane < 2, lane == NY - 1, lane >= NY - 2
    heights = [(sub.astype(jnp.float32) + (8 * zt + 0.5)) / NZ for zt in range(ZT)]

    def x_copy(sec, grp, case, way):
        buf = (s0, s1)[sec]
        c, n = GROUPS[grp]
        a, b, peer = ((NX, 0, up), (2, NX + 2, down))[way]
        return pltpu.make_async_remote_copy(
            src_ref=buf.at[case, pl.ds(c, n), pl.ds(a, 2), pl.ds(Z0, NZ), :],
            dst_ref=buf.at[case, pl.ds(c, n), pl.ds(b, 2), pl.ds(Z0, NZ), :],
            send_sem=xsend_sem.at[sec, grp, case, way],
            recv_sem=xrecv_sem.at[sec, grp, case, way],
            device_id=peer, device_id_type=MESH)

    def y_copy(sec, grp, case, way):
        c, n = GROUPS[grp]
        dst, peer = ((yleft, right), (yright, left))[way]
        return pltpu.make_async_remote_copy(
            src_ref=ysend.at[sec, case, pl.ds(c, n)],
            dst_ref=dst.at[sec, case, pl.ds(c, n)],
            send_sem=ysend_sem.at[sec, grp, case, way],
            recv_sem=yrecv_sem.at[sec, grp, case, way],
            device_id=peer, device_id_type=MESH)

    def x_start(sec, grp, case):
        for way, ok in ((0, has_up), (1, has_down)):
            @pl.when(ok)
            def _(way=way):
                x_copy(sec, grp, case, way).start()

    def y_start(sec, grp, case):
        for way, ok in ((0, has_right), (1, has_left)):
            @pl.when(ok)
            def _(way=way):
                y_copy(sec, grp, case, way).start()

    def x_wait(sec, grp, case):
        for way, ok in ((0, has_down), (1, has_up)):
            @pl.when(ok)
            def _(way=way):
                x_copy(sec, grp, case, way).wait_recv()

    def y_wait(sec, grp, case):
        for way, ok in ((0, has_left), (1, has_right)):
            @pl.when(ok)
            def _(way=way):
                y_copy(sec, grp, case, way).wait_recv()

    def packed(acc, tile, q):
        return jnp.where(lane4 == q, pltpu.roll(tile, 4 * q + 2, 1), acc)

    def time_rows(sec, case, comps, first, count):
        buf = (s0, s1)[sec]

        def body(i, _):
            x = first + i

            def row(k):
                return jnp.broadcast_to(coef[case, k, pl.ds(x, 1), :], (8, NY))

            step, slope, couple = row(STEP), row(SLOPE), row(COUPLE)
            use_y = set(comps) | ({2} if 0 in comps else set()) | ({0} if 2 in comps else set())
            ghosts = {c: jnp.where(lo_half, yleft[sec, case, c], yright[sec, case, c]) for c in sorted(use_y)}
            packs = {}
            total = bend = None
            for zt in range(ZT):
                zs = Z0 + 8 * zt
                q = x * ZT + zt
                carry = slope * heights[zt]

                def at(c, dx=0, dz=0):
                    return buf[case, c, x + 2 + dx, zs + dz:zs + dz + 8, :]

                xd, yd, e1, e2 = {}, {}, {}, {}
                for c in sorted(set(comps) | ({1} if 0 in comps else set()) | ({0} if 1 in comps else set())):
                    p1, m1, p2, m2 = at(c, 1), at(c, -1), at(c, 2), at(c, -2)
                    xd[c] = 8.0 * (p1 - m1) - (p2 - m2)
                    e1[c], e2[c] = p1 + m1, p2 + m2
                for c in sorted(use_y):
                    f = at(c)
                    ghost = pltpu.roll(ghosts[c], NY - 2 - 4 * q, 1)
                    p1 = pltpu.roll(jnp.where(first1, ghost, f), NY - 1, 1)
                    p2 = pltpu.roll(jnp.where(first2, ghost, f), NY - 2, 1)
                    m1 = pltpu.roll(jnp.where(last1, ghost, f), 1, 1)
                    m2 = pltpu.roll(jnp.where(last2, ghost, f), 2, 1)
                    if c in (0, 2):
                        yd[c] = 8.0 * (p1 - m1) - (p2 - m2)
                    if c in comps:
                        e1[c], e2[c] = e1[c] + (p1 + m1), e2[c] + (p2 + m2)
                for c in comps:
                    f = at(c)
                    new = row(CROW[c]) * f + row(AROW[c]) * (16.0 * e1[c] - e2[c])
                    new = new + row(BROW[c]) * (at(c, 0, 1) + at(c, 0, -1))
                    new = new + (carry * xd[c] + step * src[case, c, x, 8 * zt:8 * zt + 8, :])
                    if c == 0:
                        new = new + couple * (xd[1] + yd[2])
                    elif c == 1:
                        new = new + couple * xd[0]
                    elif c == 2:
                        new = new + couple * yd[0]
                    else:
                        new = new + row(HEAT) * at(1)
                    if sec == 0:
                        s1[case, c, x + 2, zs:zs + 8, :] = new
                        packs[c] = packed(packs.get(c, ysend[1, case, c]), new, q)
                    else:
                        src[case, c, x, 8 * zt:8 * zt + 8, :] = new
                        if c == 1:
                            fin[case, x, zs:zs + 8, :] = new
                        if c == 0:
                            total = new if total is None else total + new
            for c, value in packs.items():
                ysend[1, case, c] = value
            if total is not None:
                mean[x + 2, case:case + 1, :] = jnp.sum(total, axis=0, keepdims=True)
            if sec == 1 and 1 in comps:
                for zt in range(ZT):
                    zs = Z0 + 8 * zt
                    f = fin[case, x, zs:zs + 8, :]
                    term = f * (fin[case, x, zs + 1:zs + 9, :] - 2.0 * f + fin[case, x, zs - 1:zs + 7, :])
                    bend = term if bend is None else bend + term
                curv[case, pl.ds(x, 1), :] = jnp.sum(bend, axis=0, keepdims=True)
            return 0

        lax.fori_loop(0, count, body, 0)

    for copy in loads:
        copy.wait()
    for case in range(CASES):
        for c in range(NC):
            ysend[1, case, c] = zero8
    for case in range(CASES):
        def pack_row(i, accs, case=case):
            accs = list(accs)
            for c in range(NC):
                for zt in range(ZT):
                    tile = s0[case, c, i + 2, Z0 + 8 * zt:Z0 + 8 * zt + 8, :]
                    accs[c] = packed(accs[c], tile, i * ZT + zt)
            return tuple(accs)
        accs = lax.fori_loop(0, NX, pack_row, (zero8,) * NC)
        for c in range(NC):
            ysend[0, case, c] = accs[c]
    pl.semaphore_wait(barrier, plane_n - 1 + ZRING - 1 + 2)
    for case in range(CASES):
        y_start(0, 0, case)
        x_start(0, 0, case)
    for case in range(CASES):
        y_start(0, 1, case)
        x_start(0, 1, case)

    for copy in src_loads:
        copy.wait()
    for case in range(CASES):
        y_wait(0, 0, case)
        time_rows(0, case, (0, 1, 2), 2, NX - 4)
    for case in range(CASES):
        x_wait(0, 0, case)
        time_rows(0, case, (0, 1, 2), 0, 2)
        time_rows(0, case, (0, 1, 2), NX - 2, 2)
        y_start(1, 0, case)
        x_start(1, 0, case)
    for case in range(CASES):
        y_wait(0, 1, case)
        x_wait(0, 1, case)
        time_rows(0, case, (3,), 0, NX)
        y_start(1, 1, case)
        x_start(1, 1, case)

    def store_out(c, case):
        copies = []
        for x in range(NX):
            copies.append(pltpu.make_async_copy(
                src.at[case, c, x], out.at[c, case, :, x, :], out_sem.at[c, case, x]))
        return copies

    for case in range(CASES):
        y_wait(1, 0, case)
        x_wait(1, 0, case)
        time_rows(1, case, (0,), 0, NX)

    def m_copy(way):
        a, b, peer = ((NX, 0, up), (2, NX + 2, down))[way]
        return pltpu.make_async_remote_copy(
            src_ref=mean.at[pl.ds(a, 2)], dst_ref=mean.at[pl.ds(b, 2)],
            send_sem=msend_sem.at[way], recv_sem=mrecv_sem.at[way],
            device_id=peer, device_id_type=MESH)

    for way, ok in ((0, has_up), (1, has_down)):
        @pl.when(ok)
        def _(way=way):
            m_copy(way).start()
    for case in range(CASES):
        time_rows(1, case, (1,), 0, NX)
        for c in (0, 1):
            for copy in store_out(c, case):
                copy.start()
    for way, ok in ((0, has_down), (1, has_up)):
        @pl.when(ok)
        def _(way=way):
            m_copy(way).wait_recv()

    grad = jnp.zeros((NX, NY), jnp.float32)
    for case in range(CASES):
        theta = THETA_STEP * temp[case].astype(jnp.float32)
        visc = jnp.exp(VISCOSITY_PRESS * pressure[case] - VISCOSITY_TEMP * theta)
        density = 1.0 - 0.6 * cavity[case].astype(jnp.float32)

        def rows(dx):
            return mean[2 + dx:2 + dx + NX, case, :]

        slope = (8.0 * (rows(1) - rows(-1)) - (rows(2) - rows(-2))) / (12.0 * NZ)
        grad = grad + (density * thick / 2.0 * slope
                       - 8.0 * visc / (thick * thick * thick) * (curv[case] / NZ))
    wall[...] = grad
    mine[0] = jnp.sum(grad * grad, axis=0, keepdims=True)

    def plane_copy(o):
        return pltpu.make_async_remote_copy(
            src_ref=mine.at[0], dst_ref=plane.at[o], send_sem=rsend_sem.at[0], recv_sem=rrecv_sem.at[0],
            device_id=plane_peer(o), device_id_type=MESH)

    def ring_copy(o):
        return pltpu.make_async_remote_copy(
            src_ref=mine2.at[0], dst_ref=ring.at[o], send_sem=rsend_sem.at[1], recv_sem=rrecv_sem.at[1],
            device_id=ring_peer(o), device_id_type=MESH)

    for o in range(1, plane_n):
        plane_copy(o).start()
    for case in range(CASES):
        time_rows(1, case, (2,), 0, NX)
    everyone = pltpu.make_async_copy(plane.at[pl.ds(1, plane_n - 1)], plane.at[pl.ds(1, plane_n - 1)], rrecv_sem.at[0])
    everyone.wait()
    mine2[0] = mine[0] + jnp.sum(plane[1:plane_n], axis=0)
    for o in range(1, ZRING):
        ring_copy(o).start()
    for case in range(CASES):
        for copy in store_out(2, case):
            copy.start()
    for case in range(CASES):
        y_wait(1, 1, case)
        x_wait(1, 1, case)
        time_rows(1, case, (3,), 0, NX)
        for copy in store_out(3, case):
            copy.start()
    pltpu.make_async_copy(ring.at[pl.ds(1, ZRING - 1)], ring.at[pl.ds(1, ZRING - 1)], rrecv_sem.at[1]).wait()
    total = jnp.sum(mine2[0] + jnp.sum(ring[1:ZRING], axis=0), axis=1, keepdims=True)
    wall[...] = wall[...] / jnp.sqrt(total / cells + 1e-06)

    pltpu.make_async_copy(plane.at[pl.ds(1, plane_n - 1)], plane.at[pl.ds(1, plane_n - 1)], rsend_sem.at[0]).wait()
    pltpu.make_async_copy(ring.at[pl.ds(1, ZRING - 1)], ring.at[pl.ds(1, ZRING - 1)], rsend_sem.at[1]).wait()
    for way, okx, oky in ((0, has_up, has_right), (1, has_down, has_left)):
        @pl.when(okx)
        def _(way=way):
            m_copy(way).wait_send()
            for sec in range(2):
                for grp in range(2):
                    for case in range(CASES):
                        x_copy(sec, grp, case, way).wait_send()

        @pl.when(oky)
        def _(way=way):
            for sec in range(2):
                for grp in range(2):
                    for case in range(CASES):
                        y_copy(sec, grp, case, way).wait_send()
    for c in range(NC):
        for case in range(CASES):
            for copy in store_out(c, case):
                copy.wait()


def on_device(adjoint, source, pressure, film, cavity, temp_index):
    vmem = pl.BlockSpec(memory_space=pltpu.VMEM)
    hbm = pl.BlockSpec(memory_space=pl.ANY)
    smem = pl.BlockSpec(memory_space=pltpu.SMEM)
    f32 = jnp.float32
    dma = pltpu.SemaphoreType.DMA
    return pl.pallas_call(
        kernel,
        out_shape=(
            jax.ShapeDtypeStruct(adjoint.shape, f32),
            jax.ShapeDtypeStruct(film.shape, f32),
        ),
        in_specs=[hbm, hbm, vmem, vmem, vmem, smem],
        out_specs=(hbm, vmem),
        scratch_shapes=[
            pltpu.VMEM((CASES, NC, NX + 4, ZROWS, NY), f32),
            pltpu.VMEM((CASES, NC, NX + 4, ZROWS, NY), f32),
            pltpu.VMEM((CASES, NX, ZROWS, NY), f32),
            pltpu.VMEM((CASES, NC, NX, NZ, NY), f32),
            pltpu.VMEM((CASES, 13, NX, NY), f32),
            pltpu.VMEM((2, CASES, NC, 8, NY), f32),
            pltpu.VMEM((2, CASES, NC, 8, NY), f32),
            pltpu.VMEM((2, CASES, NC, 8, NY), f32),
            pltpu.VMEM((NX + 4, CASES, NY), f32),
            pltpu.VMEM((CASES, NX, NY), f32),
            pltpu.VMEM((1, 1, NY), f32),
            pltpu.VMEM((32, 1, NY), f32),
            pltpu.VMEM((1, 1, NY), f32),
            pltpu.VMEM((ZRING, 1, NY), f32),
            dma((CASES, NX)),
            dma((CASES, NX)),
            dma((NC, CASES, NX)),
            dma((2, 2, CASES, 2)),
            dma((2, 2, CASES, 2)),
            dma((2, 2, CASES, 2)),
            dma((2, 2, CASES, 2)),
            dma((2,)),
            dma((2,)),
            dma((2,)),
            dma((2,)),
        ],
        compiler_params=pltpu.CompilerParams(
            collective_id=0, has_side_effects=True, vmem_limit_bytes=48 * 1024 * 1024
        ),
        name="lubrication_adjoint",
    )(adjoint, source, pressure, film, cavity, temp_index)


def solution(mesh):
    placed = (
        P(None, None, None, "roll", "trans"),
        P(None, None, None, "roll", "trans"),
        P(None, "roll", "trans"),
        P("roll", "trans"),
        P(None, "roll", "trans"),
        P(),
    )
    return jax.shard_map(
        on_device,
        mesh=mesh,
        in_specs=placed,
        out_specs=(P(None, None, None, "roll", "trans"), P("roll", "trans")),
        check_vma=False,
    )
```

```python
import jax
import jax.numpy as jnp
from jax import lax
from jax.experimental import pallas as pl
from jax.experimental.pallas import tpu as pltpu
from jax.sharding import PartitionSpec as P

VISCOSITY_PRESS = 0.3
VISCOSITY_TEMP = 0.5
THETA_STEP = 0.2
SOUND = 0.5
KAPPA = 0.6
HEATING = 0.3
COURANT = 0.8

MESH = pl.DeviceIdType.MESH
NC = 4
CASES = 2
NZ = 32
NX = 8
NY = 128
Z0 = 8
ZROWS = 48
ZT = NZ // 8
ZRING = 8
XGROUPS = (((0, 3), (3, 1)), ((0, 2), (2, 2)))
YGROUPS = (((0, 3), (3, 1)), ((0, 3), (3, 1)))

STEP, SLOPE, COUPLE, HEAT, A0, A1, A3, B0, B1, B3, C0, C1, C3 = range(13)
AROW = (A0, A1, A1, A3)
BROW = (B0, B1, B1, B3)
CROW = (C0, C1, C1, C3)


def kernel(
    adjoint, source, pressure_in, film_in, cavity_in, temp_in, out, wall,
    pressure, film, cavity, temp,
    s0, s1, fin, src, coef, ysend, yleft, yright, mean, curv, mine, plane, mine2, ring,
    small_sem, in_sem, src_sem, out_sem, xsend_sem, xrecv_sem, ysend_sem, yrecv_sem,
    msend_sem, mrecv_sem, rsend_sem, rrecv_sem,
):
    nr, nt = lax.axis_size("roll"), lax.axis_size("trans")
    r, t = lax.axis_index("roll"), lax.axis_index("trans")
    core = lax.rem(r, 2)
    z = lax.rem(r // 2, ZRING)
    g = r // (2 * ZRING)
    groups = nr // (2 * ZRING)
    plane_n = groups * 2 * nt
    cells = nr * NX * nt * NY

    def plane_peer(o):
        dt, dg, dc = o // (2 * groups), (o // 2) % groups, o % 2
        row = (lax.rem(g + dg, groups) * ZRING + z) * 2 + lax.rem(core + dc, 2)
        return (row, lax.rem(t + dt, nt))

    def ring_peer(o):
        return ((g * ZRING + lax.rem(z + o, ZRING)) * 2 + core, t)

    up = (lax.rem(r + 1, nr), t)
    down = (lax.rem(r + nr - 1, nr), t)
    right = (r, lax.rem(t + 1, nt))
    left = (r, lax.rem(t + nt - 1, nt))
    has_up, has_down = r < nr - 1, r > 0
    has_right, has_left = t < nt - 1, t > 0

    barrier = pltpu.get_barrier_semaphore()
    for o in range(1, plane_n):
        pl.semaphore_signal(barrier, inc=1, device_id=plane_peer(o), device_id_type=MESH)
    for o in range(1, ZRING):
        pl.semaphore_signal(barrier, inc=1, device_id=ring_peer(o), device_id_type=MESH)
    for peer in (up, down):
        pl.semaphore_signal(barrier, inc=1, device_id=peer, device_id_type=MESH)

    smalls = [
        pltpu.make_async_copy(given, held, small_sem.at[k])
        for k, (given, held) in enumerate(
            ((pressure_in, pressure), (film_in, film), (cavity_in, cavity), (temp_in, temp)))
    ]
    for copy in smalls:
        copy.start()
    loads, src_loads = [], []
    for case in range(CASES):
        for x in range(NX):
            loads.append(pltpu.make_async_copy(
                adjoint.at[:, case, :, x, :], s0.at[case, :, 2 + x, Z0:Z0 + NZ, :], in_sem.at[case, x]))
            src_loads.append(pltpu.make_async_copy(
                source.at[:, case, :, x, :], src.at[case, :, x], src_sem.at[case, x]))
    for copy in loads:
        copy.start()
    for copy in src_loads:
        copy.start()

    for copy in smalls:
        copy.wait()
    thick = film[...]
    for case in range(CASES):
        theta = THETA_STEP * temp[case].astype(jnp.float32)
        visc = jnp.exp(VISCOSITY_PRESS * pressure[case] - VISCOSITY_TEMP * theta)
        fcoef = 4.0 * visc / (thick * thick)
        density = 1.0 - 0.6 * cavity[case].astype(jnp.float32)
        step = COURANT / (32.0 / 3.0 * visc + 4.0 * fcoef + 2.0 * SOUND + 1.0)
        sv, sf = step * visc, step * fcoef
        rows = {
            STEP: step, SLOPE: step * density / 12.0, COUPLE: step * (SOUND / 12.0), HEAT: HEATING * sv,
        }
        for scale, a, b, c in ((0.5, A0, B0, C0), (1.0, A1, B1, C1), (KAPPA, A3, B3, C3)):
            rows[a] = (scale / 12.0) * sv
            rows[b] = scale * sf
            rows[c] = 1.0 - scale * (5.0 * sv + 2.0 * sf)
        for k, value in rows.items():
            coef[case, k] = value

    zero8 = jnp.zeros((8, NY), jnp.float32)
    for buf in (s0, s1):
        for case in range(CASES):
            def clear(i, _, buf=buf, case=case):
                for c in range(NC):
                    buf[case, c, i, 0:Z0, :] = zero8
                    buf[case, c, i, Z0 + NZ:ZROWS, :] = zero8
                return 0
            lax.fori_loop(0, NX + 4, clear, 0)
    for case in range(CASES):
        def clear(i, _, case=case):
            fin[case, i, 0:Z0, :] = zero8
            fin[case, i, Z0 + NZ:ZROWS, :] = zero8
            return 0
        lax.fori_loop(0, NX, clear, 0)

    def clear_slab(first):
        for buf in (s0, s1):
            for case in range(CASES):
                for c in range(NC):
                    for x in (first, first + 1):
                        buf[case, c, x, Z0:Z0 + NZ, :] = jnp.zeros((NZ, NY), jnp.float32)

    @pl.when(jnp.logical_not(has_down))
    def _():
        clear_slab(0)
        mean[0:2] = jnp.zeros((2, CASES, NY), jnp.float32)

    @pl.when(jnp.logical_not(has_up))
    def _():
        clear_slab(NX + 2)
        mean[NX + 2:NX + 4] = jnp.zeros((2, CASES, NY), jnp.float32)

    @pl.when(jnp.logical_not(has_left))
    def _():
        yleft[...] = jnp.zeros(yleft.shape, jnp.float32)

    @pl.when(jnp.logical_not(has_right))
    def _():
        yright[...] = jnp.zeros(yright.shape, jnp.float32)

    lane = lax.broadcasted_iota(jnp.int32, (8, NY), 1)
    sub = lax.broadcasted_iota(jnp.int32, (8, NY), 0)
    lane4 = lane // 4
    lo_half = lane % 4 < 2
    first1, first2, last1, last2 = lane == 0, lane < 2, lane == NY - 1, lane >= NY - 2
    heights = [(sub.astype(jnp.float32) + (8 * zt + 0.5)) / NZ for zt in range(ZT)]

    def x_copy(sec, grp, case, way):
        buf = (s0, s1)[sec]
        c, n = XGROUPS[sec][grp]
        a, b, peer = ((NX, 0, up), (2, NX + 2, down))[way]
        return pltpu.make_async_remote_copy(
            src_ref=buf.at[case, pl.ds(c, n), pl.ds(a, 2), pl.ds(Z0, NZ), :],
            dst_ref=buf.at[case, pl.ds(c, n), pl.ds(b, 2), pl.ds(Z0, NZ), :],
            send_sem=xsend_sem.at[sec, grp, case, way],
            recv_sem=xrecv_sem.at[sec, grp, case, way],
            device_id=peer, device_id_type=MESH)

    def y_copy(sec, grp, case, way):
        c, n = YGROUPS[sec][grp]
        dst, peer = ((yleft, right), (yright, left))[way]
        return pltpu.make_async_remote_copy(
            src_ref=ysend.at[sec, case, pl.ds(c, n)],
            dst_ref=dst.at[sec, case, pl.ds(c, n)],
            send_sem=ysend_sem.at[sec, grp, case, way],
            recv_sem=yrecv_sem.at[sec, grp, case, way],
            device_id=peer, device_id_type=MESH)

    def x_start(sec, grp, case):
        for way, ok in ((0, has_up), (1, has_down)):
            @pl.when(ok)
            def _(way=way):
                x_copy(sec, grp, case, way).start()

    def y_start(sec, grp, case):
        for way, ok in ((0, has_right), (1, has_left)):
            @pl.when(ok)
            def _(way=way):
                y_copy(sec, grp, case, way).start()

    def x_wait(sec, grp, case):
        for way, ok in ((0, has_down), (1, has_up)):
            @pl.when(ok)
            def _(way=way):
                x_copy(sec, grp, case, way).wait_recv()

    def y_wait(sec, grp, case):
        for way, ok in ((0, has_left), (1, has_right)):
            @pl.when(ok)
            def _(way=way):
                y_copy(sec, grp, case, way).wait_recv()

    def packed(acc, tile, q):
        return jnp.where(lane4 == q, pltpu.roll(tile, 4 * q + 2, 1), acc)

    def time_rows(sec, case, comps, first, count):
        buf = (s0, s1)[sec]

        def body(i, _):
            x = first + i

            def row(k):
                return jnp.broadcast_to(coef[case, k, pl.ds(x, 1), :], (8, NY))

            step, slope, couple = row(STEP), row(SLOPE), row(COUPLE)
            use_y = set(comps) | ({2} if 0 in comps else set()) | ({0} if 2 in comps else set())
            ghosts = {c: jnp.where(lo_half, yleft[sec, case, c], yright[sec, case, c]) for c in sorted(use_y)}
            packs = {}
            total = bend = None
            for zt in range(ZT):
                zs = Z0 + 8 * zt
                q = x * ZT + zt
                carry = slope * heights[zt]

                def at(c, dx=0, dz=0):
                    return buf[case, c, x + 2 + dx, zs + dz:zs + dz + 8, :]

                xd, yd, e1, e2 = {}, {}, {}, {}
                for c in sorted(set(comps) | ({1} if 0 in comps else set()) | ({0} if 1 in comps else set())):
                    p1, m1, p2, m2 = at(c, 1), at(c, -1), at(c, 2), at(c, -2)
                    xd[c] = 8.0 * (p1 - m1) - (p2 - m2)
                    e1[c], e2[c] = p1 + m1, p2 + m2
                for c in sorted(use_y):
                    f = at(c)
                    ghost = pltpu.roll(ghosts[c], NY - 2 - 4 * q, 1)
                    p1 = pltpu.roll(jnp.where(first1, ghost, f), NY - 1, 1)
                    p2 = pltpu.roll(jnp.where(first2, ghost, f), NY - 2, 1)
                    m1 = pltpu.roll(jnp.where(last1, ghost, f), 1, 1)
                    m2 = pltpu.roll(jnp.where(last2, ghost, f), 2, 1)
                    if c in (0, 2):
                        yd[c] = 8.0 * (p1 - m1) - (p2 - m2)
                    if c in comps:
                        e1[c], e2[c] = e1[c] + (p1 + m1), e2[c] + (p2 + m2)
                for c in comps:
                    f = at(c)
                    new = row(CROW[c]) * f + row(AROW[c]) * (16.0 * e1[c] - e2[c])
                    new = new + row(BROW[c]) * (at(c, 0, 1) + at(c, 0, -1))
                    new = new + (carry * xd[c] + step * src[case, c, x, 8 * zt:8 * zt + 8, :])
                    if c == 0:
                        new = new + couple * (xd[1] + yd[2])
                    elif c == 1:
                        new = new + couple * xd[0]
                    elif c == 2:
                        new = new + couple * yd[0]
                    else:
                        new = new + row(HEAT) * at(1)
                    if sec == 0:
                        s1[case, c, x + 2, zs:zs + 8, :] = new
                        packs[c] = packed(packs.get(c, ysend[1, case, c]), new, q)
                    else:
                        src[case, c, x, 8 * zt:8 * zt + 8, :] = new
                        if c == 1:
                            fin[case, x, zs:zs + 8, :] = new
                        if c == 0:
                            total = new if total is None else total + new
            for c, value in packs.items():
                ysend[1, case, c] = value
            if total is not None:
                mean[x + 2, case:case + 1, :] = jnp.sum(total, axis=0, keepdims=True)
            if sec == 1 and 1 in comps:
                for zt in range(ZT):
                    zs = Z0 + 8 * zt
                    f = fin[case, x, zs:zs + 8, :]
                    term = f * (fin[case, x, zs + 1:zs + 9, :] - 2.0 * f + fin[case, x, zs - 1:zs + 7, :])
                    bend = term if bend is None else bend + term
                curv[case, pl.ds(x, 1), :] = jnp.sum(bend, axis=0, keepdims=True)
            return 0

        lax.fori_loop(0, count, body, 0)

    for copy in loads:
        copy.wait()
    for case in range(CASES):
        for c in range(NC):
            ysend[1, case, c] = zero8
    for case in range(CASES):
        def pack_row(i, accs, case=case):
            accs = list(accs)
            for c in range(NC):
                for zt in range(ZT):
                    tile = s0[case, c, i + 2, Z0 + 8 * zt:Z0 + 8 * zt + 8, :]
                    accs[c] = packed(accs[c], tile, i * ZT + zt)
            return tuple(accs)
        accs = lax.fori_loop(0, NX, pack_row, (zero8,) * NC)
        for c in range(NC):
            ysend[0, case, c] = accs[c]
    pl.semaphore_wait(barrier, plane_n - 1 + ZRING - 1 + 2)
    for case in range(CASES):
        y_start(0, 0, case)
        x_start(0, 0, case)

    for copy in src_loads:
        copy.wait()
    for case in range(CASES):
        y_wait(0, 0, case)
        time_rows(0, case, (0, 1, 2), 2, NX - 4)
    for case in range(CASES):
        x_wait(0, 0, case)
        time_rows(0, case, (0, 1, 2), 0, 2)
        time_rows(0, case, (0, 1, 2), NX - 2, 2)
        y_start(1, 0, case)
        x_start(1, 0, case)
    for case in range(CASES):
        y_start(0, 1, case)
        x_start(0, 1, case)

    def store_out(c, case):
        copies = []
        for x in range(NX):
            copies.append(pltpu.make_async_copy(
                src.at[case, c, x], out.at[c, case, :, x, :], out_sem.at[c, case, x]))
        return copies

    for case in range(CASES):
        y_wait(1, 0, case)
        x_wait(1, 0, case)
        time_rows(1, case, (0,), 0, NX)

    def m_copy(way):
        a, b, peer = ((NX, 0, up), (2, NX + 2, down))[way]
        return pltpu.make_async_remote_copy(
            src_ref=mean.at[pl.ds(a, 2)], dst_ref=mean.at[pl.ds(b, 2)],
            send_sem=msend_sem.at[way], recv_sem=mrecv_sem.at[way],
            device_id=peer, device_id_type=MESH)

    for way, ok in ((0, has_up), (1, has_down)):
        @pl.when(ok)
        def _(way=way):
            m_copy(way).start()
    for case in range(CASES):
        time_rows(1, case, (1,), 0, NX)
        for c in (0, 1):
            for copy in store_out(c, case):
                copy.start()
    for way, ok in ((0, has_down), (1, has_up)):
        @pl.when(ok)
        def _(way=way):
            m_copy(way).wait_recv()

    grad = jnp.zeros((NX, NY), jnp.float32)
    for case in range(CASES):
        theta = THETA_STEP * temp[case].astype(jnp.float32)
        visc = jnp.exp(VISCOSITY_PRESS * pressure[case] - VISCOSITY_TEMP * theta)
        density = 1.0 - 0.6 * cavity[case].astype(jnp.float32)

        def rows(dx):
            return mean[2 + dx:2 + dx + NX, case, :]

        slope = (8.0 * (rows(1) - rows(-1)) - (rows(2) - rows(-2))) / (12.0 * NZ)
        grad = grad + (density * thick / 2.0 * slope
                       - 8.0 * visc / (thick * thick * thick) * (curv[case] / NZ))
    wall[...] = grad
    mine[0] = jnp.sum(grad * grad, axis=0, keepdims=True)

    def plane_copy(o):
        return pltpu.make_async_remote_copy(
            src_ref=mine.at[0], dst_ref=plane.at[o], send_sem=rsend_sem.at[0], recv_sem=rrecv_sem.at[0],
            device_id=plane_peer(o), device_id_type=MESH)

    def ring_copy(o):
        return pltpu.make_async_remote_copy(
            src_ref=mine2.at[0], dst_ref=ring.at[o], send_sem=rsend_sem.at[1], recv_sem=rrecv_sem.at[1],
            device_id=ring_peer(o), device_id_type=MESH)

    for o in range(1, plane_n):
        plane_copy(o).start()
    for case in range(CASES):
        y_wait(0, 1, case)
        x_wait(0, 1, case)
        time_rows(0, case, (3,), 0, NX)
        y_start(1, 1, case)
        x_start(1, 1, case)

    everyone = pltpu.make_async_copy(plane.at[pl.ds(1, plane_n - 1)], plane.at[pl.ds(1, plane_n - 1)], rrecv_sem.at[0])
    everyone.wait()
    mine2[0] = mine[0] + jnp.sum(plane[1:plane_n], axis=0)
    for o in range(1, ZRING):
        ring_copy(o).start()
    for case in range(CASES):
        y_wait(1, 1, case)
        x_wait(1, 1, case)
        time_rows(1, case, (2, 3), 0, NX)
        for c in (2, 3):
            for copy in store_out(c, case):
                copy.start()
    pltpu.make_async_copy(ring.at[pl.ds(1, ZRING - 1)], ring.at[pl.ds(1, ZRING - 1)], rrecv_sem.at[1]).wait()
    total = jnp.sum(mine2[0] + jnp.sum(ring[1:ZRING], axis=0), axis=1, keepdims=True)
    wall[...] = wall[...] / jnp.sqrt(total / cells + 1e-06)

    pltpu.make_async_copy(plane.at[pl.ds(1, plane_n - 1)], plane.at[pl.ds(1, plane_n - 1)], rsend_sem.at[0]).wait()
    pltpu.make_async_copy(ring.at[pl.ds(1, ZRING - 1)], ring.at[pl.ds(1, ZRING - 1)], rsend_sem.at[1]).wait()
    for way, okx, oky in ((0, has_up, has_right), (1, has_down, has_left)):
        @pl.when(okx)
        def _(way=way):
            m_copy(way).wait_send()
            for sec in range(2):
                for grp in range(2):
                    for case in range(CASES):
                        x_copy(sec, grp, case, way).wait_send()

        @pl.when(oky)
        def _(way=way):
            for sec in range(2):
                for grp in range(2):
                    for case in range(CASES):
                        y_copy(sec, grp, case, way).wait_send()
    for c in range(NC):
        for case in range(CASES):
            for copy in store_out(c, case):
                copy.wait()


def on_device(adjoint, source, pressure, film, cavity, temp_index):
    vmem = pl.BlockSpec(memory_space=pltpu.VMEM)
    hbm = pl.BlockSpec(memory_space=pltpu.HBM)
    f32 = jnp.float32
    dma = pltpu.SemaphoreType.DMA
    given = [
        pltpu.with_memory_space_constraint(a, pltpu.HBM)
        for a in (adjoint, source, pressure, film, cavity, temp_index)
    ]
    return pl.pallas_call(
        kernel,
        out_shape=(pltpu.VMEM(adjoint.shape, f32), pltpu.VMEM(film.shape, f32)),
        in_specs=[hbm] * 6,
        out_specs=(vmem, vmem),
        scratch_shapes=[
            pltpu.VMEM(pressure.shape, f32),
            pltpu.VMEM(film.shape, f32),
            pltpu.VMEM(cavity.shape, jnp.int32),
            pltpu.SMEM(temp_index.shape, jnp.int32),
            pltpu.VMEM((CASES, NC, NX + 4, ZROWS, NY), f32),
            pltpu.VMEM((CASES, NC, NX + 4, ZROWS, NY), f32),
            pltpu.VMEM((CASES, NX, ZROWS, NY), f32),
            pltpu.VMEM((CASES, NC, NX, NZ, NY), f32),
            pltpu.VMEM((CASES, 13, NX, NY), f32),
            pltpu.VMEM((2, CASES, NC, 8, NY), f32),
            pltpu.VMEM((2, CASES, NC, 8, NY), f32),
            pltpu.VMEM((2, CASES, NC, 8, NY), f32),
            pltpu.VMEM((NX + 4, CASES, NY), f32),
            pltpu.VMEM((CASES, NX, NY), f32),
            pltpu.VMEM((1, 1, NY), f32),
            pltpu.VMEM((32, 1, NY), f32),
            pltpu.VMEM((1, 1, NY), f32),
            pltpu.VMEM((ZRING, 1, NY), f32),
            dma((4,)),
            dma((CASES, NX)),
            dma((CASES, NX)),
            dma((NC, CASES, NX)),
            dma((2, 2, CASES, 2)),
            dma((2, 2, CASES, 2)),
            dma((2, 2, CASES, 2)),
            dma((2, 2, CASES, 2)),
            dma((2,)),
            dma((2,)),
            dma((2,)),
            dma((2,)),
        ],
        compiler_params=pltpu.CompilerParams(
            collective_id=0, has_side_effects=True, vmem_limit_bytes=48 * 1024 * 1024
        ),
        name="lubrication_adjoint",
    )(*given)


def solution(mesh):
    placed = (
        P(None, None, None, "roll", "trans"),
        P(None, None, None, "roll", "trans"),
        P(None, "roll", "trans"),
        P("roll", "trans"),
        P(None, "roll", "trans"),
        P(),
    )
    return jax.shard_map(
        on_device,
        mesh=mesh,
        in_specs=placed,
        out_specs=(P(None, None, None, "roll", "trans"), P("roll", "trans")),
        check_vma=False,
    )
```

```python
import jax
import jax.numpy as jnp
from jax import lax
from jax.experimental import pallas as pl
from jax.experimental.pallas import tpu as pltpu
from jax.sharding import PartitionSpec as P

VISCOSITY_PRESS = 0.3
VISCOSITY_TEMP = 0.5
THETA_STEP = 0.2
SOUND = 0.5
KAPPA = 0.6
HEATING = 0.3
COURANT = 0.8

MESH = pl.DeviceIdType.MESH
NC = 4
CASES = 2
NZ = 32
NX = 8
NY = 128
Z0 = 8
ZROWS = 48
ZT = NZ // 8
ZRING = 8
XGROUPS = (((0, 3), (3, 1)), ((0, 2), (2, 2)))
YGROUPS = (((0, 3), (3, 1)), ((0, 3), (3, 1)))

STEP, SLOPE, COUPLE, HEAT, A0, A1, A3, B0, B1, B3, C0, C1, C3 = range(13)
AROW = (A0, A1, A1, A3)
BROW = (B0, B1, B1, B3)
CROW = (C0, C1, C1, C3)


def kernel(
    adjoint, source, pressure_in, film_in, cavity_in, temp_in, out, wall,
    pressure, film, cavity, temp,
    s0, s1, halo, src, coef, pcoef, ysend, yleft, yright, mean, curv, mine, plane, mine2, ring,
    small_sem, in_sem, src_sem, out_sem, xsend_sem, xrecv_sem, ysend_sem, yrecv_sem,
    msend_sem, mrecv_sem, rsend_sem, rrecv_sem,
):
    nr, nt = lax.axis_size("roll"), lax.axis_size("trans")
    r, t = lax.axis_index("roll"), lax.axis_index("trans")
    core = lax.rem(r, 2)
    z = lax.rem(r // 2, ZRING)
    g = r // (2 * ZRING)
    groups = nr // (2 * ZRING)
    plane_n = groups * 2 * nt
    cells = nr * NX * nt * NY

    def plane_peer(o):
        dt, dg, dc = o // (2 * groups), (o // 2) % groups, o % 2
        row = (lax.rem(g + dg, groups) * ZRING + z) * 2 + lax.rem(core + dc, 2)
        return (row, lax.rem(t + dt, nt))

    def ring_peer(o):
        return ((g * ZRING + lax.rem(z + o, ZRING)) * 2 + core, t)

    up = (lax.rem(r + 1, nr), t)
    down = (lax.rem(r + nr - 1, nr), t)
    right = (r, lax.rem(t + 1, nt))
    left = (r, lax.rem(t + nt - 1, nt))
    has_up, has_down = r < nr - 1, r > 0
    has_right, has_left = t < nt - 1, t > 0

    barrier = pltpu.get_barrier_semaphore()
    for o in range(1, plane_n):
        pl.semaphore_signal(barrier, inc=1, device_id=plane_peer(o), device_id_type=MESH)
    for o in range(1, ZRING):
        pl.semaphore_signal(barrier, inc=1, device_id=ring_peer(o), device_id_type=MESH)
    for peer in (up, down):
        pl.semaphore_signal(barrier, inc=1, device_id=peer, device_id_type=MESH)

    smalls = [
        pltpu.make_async_copy(given, held, small_sem.at[k])
        for k, (given, held) in enumerate(
            ((pressure_in, pressure), (film_in, film), (cavity_in, cavity), (temp_in, temp)))
    ]
    loads = [
        pltpu.make_async_copy(
            adjoint.at[:, :, :, x, :], s0.at[:, :, 2 + x, pl.ds(Z0, NZ), :], in_sem.at[x])
        for x in range(NX)
    ]
    src_loads = [
        pltpu.make_async_copy(source.at[:, :, :, x, :], src.at[:, :, x], src_sem.at[x])
        for x in range(NX)
    ]
    for copy in smalls + loads + src_loads:
        copy.start()

    lane = lax.broadcasted_iota(jnp.int32, (8, NY), 1)
    sub = lax.broadcasted_iota(jnp.int32, (8, NY), 0)
    lane4, lane_in4 = lane // 4, lane % 4
    lo_half = lane_in4 < 2
    near1, near2 = lane_in4 == 1, lane_in4 == 2
    rim = jnp.logical_or(lane < 2, lane >= NY - 2)
    heights = [(sub.astype(jnp.float32) + (8 * zt + 0.5)) / NZ for zt in range(ZT)]
    zero8 = jnp.zeros((8, NY), jnp.float32)

    for buf in (s0, s1):
        def clear(i, _, buf=buf):
            for case in range(CASES):
                for c in range(NC):
                    buf[c, case, i, 0:Z0, :] = zero8
                    buf[c, case, i, Z0 + NZ:ZROWS, :] = zero8
            return 0
        lax.fori_loop(0, NX + 4, clear, 0)

        def clear_row(i, _, buf=buf):
            for case in range(CASES):
                for x in (0, 1, NX + 2, NX + 3):
                    for zt in range(ZT):
                        buf[i, case, x, Z0 + 8 * zt:Z0 + 8 * zt + 8, :] = zero8
            return 0
        lax.fori_loop(0, NC, clear_row, 0)

    def clear_pack(i, _):
        for case in range(CASES):
            for sec in range(2):
                ysend[sec, i, case] = zero8
        return 0
    lax.fori_loop(0, NC, clear_pack, 0)

    @pl.when(jnp.logical_not(has_down))
    def _():
        mean[0:2] = jnp.zeros((2, CASES, NY), jnp.float32)

    @pl.when(jnp.logical_not(has_up))
    def _():
        mean[NX + 2:NX + 4] = jnp.zeros((2, CASES, NY), jnp.float32)

    @pl.when(jnp.logical_not(has_left))
    def _():
        yleft[...] = jnp.zeros(yleft.shape, jnp.float32)

    @pl.when(jnp.logical_not(has_right))
    def _():
        yright[...] = jnp.zeros(yright.shape, jnp.float32)

    for copy in smalls:
        copy.wait()
    thick = film[...]
    for case in range(CASES):
        theta = THETA_STEP * temp[case].astype(jnp.float32)
        visc = jnp.exp(VISCOSITY_PRESS * pressure[case] - VISCOSITY_TEMP * theta)
        fcoef = 4.0 * visc / (thick * thick)
        density = 1.0 - 0.6 * cavity[case].astype(jnp.float32)
        step = COURANT / (32.0 / 3.0 * visc + 4.0 * fcoef + 2.0 * SOUND + 1.0)
        sv, sf = step * visc, step * fcoef
        table = {
            STEP: step, SLOPE: step * density / 12.0, COUPLE: step * (SOUND / 12.0), HEAT: HEATING * sv,
        }
        for scale, a, b, c in ((0.5, A0, B0, C0), (1.0, A1, B1, C1), (KAPPA, A3, B3, C3)):
            table[a] = (scale / 12.0) * sv
            table[b] = scale * sf
            table[c] = 1.0 - scale * (5.0 * sv + 2.0 * sf)
        for k, value in table.items():
            coef[case, k] = value
        for k, value in ((0, sv), (1, step)):
            acc = zero8
            for x in range(NX):
                here = jnp.logical_and(lane4 == ZT * x, sub == x)
                acc = jnp.where(here, pltpu.roll(value, 4 * ZT * x + 2, 1), acc)
            acc = acc + pltpu.roll(acc, 4, 1)
            acc = acc + pltpu.roll(acc, 8, 1)
            spread = jnp.broadcast_to(jnp.sum(acc, axis=0, keepdims=True), (8, NY))
            if k == 0:
                pcoef[case, 0] = (0.5 / 12.0) * spread
                pcoef[case, 1] = (1.0 / 12.0) * spread
                pcoef[case, 2] = (KAPPA / 12.0) * spread
            else:
                pcoef[case, 3] = (SOUND / 12.0) * spread

    def x_copy(sec, grp, case, way):
        buf = (s0, s1)[sec]
        c, n = XGROUPS[sec][grp]
        a, peer = ((NX, up), (2, down))[way]
        return pltpu.make_async_remote_copy(
            src_ref=buf.at[pl.ds(c, n), case, pl.ds(a, 2), pl.ds(Z0, NZ), :],
            dst_ref=halo.at[sec, way, case, pl.ds(c, n)],
            send_sem=xsend_sem.at[sec, grp, case, way],
            recv_sem=xrecv_sem.at[sec, grp, case, way],
            device_id=peer, device_id_type=MESH)

    def y_copy(sec, grp, case, way):
        c, n = YGROUPS[sec][grp]
        dst, peer = ((yleft, right), (yright, left))[way]
        return pltpu.make_async_remote_copy(
            src_ref=ysend.at[sec, pl.ds(c, n), case],
            dst_ref=dst.at[sec, pl.ds(c, n), case],
            send_sem=ysend_sem.at[sec, grp, case, way],
            recv_sem=yrecv_sem.at[sec, grp, case, way],
            device_id=peer, device_id_type=MESH)

    def x_start(sec, grp, case):
        for way, ok in ((0, has_up), (1, has_down)):
            @pl.when(ok)
            def _(way=way):
                x_copy(sec, grp, case, way).start()

    def y_start(sec, grp, case):
        for way, ok in ((0, has_right), (1, has_left)):
            @pl.when(ok)
            def _(way=way):
                y_copy(sec, grp, case, way).start()

    def y_wait(sec, grp, case):
        for way, ok in ((0, has_left), (1, has_right)):
            @pl.when(ok)
            def _(way=way):
                y_copy(sec, grp, case, way).wait_recv()

    def sent(copy, sec, grp, oks):
        for way in range(2):
            @pl.when(oks[way])
            def _(way=way):
                for case in range(CASES):
                    copy(sec, grp, case, way).wait_send()

    def row_of(case, k, x):
        return jnp.broadcast_to(coef[case, k, pl.ds(x, 1), :], (8, NY))

    def packed(acc, tile, q):
        return jnp.where(lane4 == q, pltpu.roll(tile, 4 * q + 2, 1), acc)

    def inner(sec, case, comps):
        cur, new_buf = ((s0, s1), (s1, s0))[sec]
        need_x = sorted(set(comps) | ({1} if 0 in comps else set()) | ({0} if 1 in comps else set()))
        need_y = sorted(set(comps) | ({2} if 0 in comps else set()) | ({0} if 2 in comps else set()))

        def body(x, _):
            def row(k):
                return row_of(case, k, x)

            step, slope, couple = row(STEP), row(SLOPE), row(COUPLE)
            packs = {}
            if sec == 0:
                packs = {(s, c): ysend[s, c, case] for c in comps for s in range(2)}
            for zt in range(ZT):
                zs = Z0 + 8 * zt
                q = x * ZT + zt
                carry = slope * heights[zt]

                def at(c, dx=0, dz=0):
                    return cur[c, case, x + 2 + dx, zs + dz:zs + dz + 8, :]

                xd, yd, e1, e2 = {}, {}, {}, {}
                for c in need_y:
                    f = at(c)
                    p1, m1 = pltpu.roll(f, NY - 1, 1), pltpu.roll(f, 1, 1)
                    p2, m2 = pltpu.roll(f, NY - 2, 1), pltpu.roll(f, 2, 1)
                    if (c == 2 and 0 in comps) or (c == 0 and 2 in comps):
                        yd[c] = 8.0 * (p1 - m1) - (p2 - m2)
                    e1[c], e2[c] = p1 + m1, p2 + m2
                    if sec == 0 and c in comps:
                        packs[0, c] = packed(packs[0, c], f, q)
                for c in need_x:
                    p1, m1, p2, m2 = at(c, 1), at(c, -1), at(c, 2), at(c, -2)
                    xd[c] = 8.0 * (p1 - m1) - (p2 - m2)
                    if c in comps:
                        e1[c], e2[c] = e1[c] + (p1 + m1), e2[c] + (p2 + m2)
                for c in comps:
                    new = row(CROW[c]) * at(c) + row(AROW[c]) * (16.0 * e1[c] - e2[c])
                    new = new + row(BROW[c]) * (at(c, 0, 1) + at(c, 0, -1))
                    new = new + (carry * xd[c] + step * src[c, case, x, 8 * zt:8 * zt + 8, :])
                    if c == 0:
                        new = new + couple * (xd[1] + yd[2])
                    elif c == 1:
                        new = new + couple * xd[0]
                    elif c == 2:
                        new = new + couple * yd[0]
                    else:
                        new = new + row(HEAT) * at(1)
                    new_buf[c, case, x + 2, zs:zs + 8, :] = new
                    if sec == 0:
                        packs[1, c] = packed(packs[1, c], new, q)
            for (s, c), value in packs.items():
                ysend[s, c, case] = value
            return 0

        lax.fori_loop(0, NX, body, 0)

    def rims(sec, case, comps):
        near, far, cross = {}, {}, {}
        for c in sorted(set(comps) | ({2} if 0 in comps else set()) | ({0} if 2 in comps else set())):
            d = jnp.where(lo_half, yleft[sec, c, case], yright[sec, c, case]) - ysend[sec, c, case]
            p1, m1 = pltpu.roll(d, NY - 1, 1), pltpu.roll(d, 1, 1)
            far_d = jnp.where(lo_half, pltpu.roll(d, NY - 2, 1), pltpu.roll(d, 2, 1))
            near[c] = 16.0 * jnp.where(near1, p1, jnp.where(near2, m1, 0.0)) - far_d
            cross[c] = 8.0 * jnp.where(near1, p1, jnp.where(near2, -m1, 0.0)) + jnp.where(lo_half, -far_d, far_d)
        result = {}
        for c in comps:
            value = pcoef[case, (0, 1, 1, 2)[c]] * near[c]
            if c in (0, 2):
                value = value + pcoef[case, 3] * cross[2 - c]
            result[c] = value
        return result

    def add_rims(sec, case, added, x):
        new_buf = (s1, s0)[sec]
        for c, value in added.items():
            for zt in range(ZT):
                zs = Z0 + 8 * zt
                here = jnp.where(rim, pltpu.roll(value, NY - 2 - 4 * (x * ZT + zt), 1), 0.0)
                new_buf[c, case, x + 2, zs:zs + 8, :] = new_buf[c, case, x + 2, zs:zs + 8, :] + here

    def edges(sec, grp, case, comps, wait=True):
        new_buf = (s1, s0)[sec]
        added = rims(sec, case, comps)
        for x in (0, 1, NX - 2, NX - 1):
            add_rims(sec, case, added, x)
        if sec == 0:
            for c in comps:
                ysend[1, c, case] = ysend[1, c, case] + added[c]
        for way, ok in ((0, has_down), (1, has_up)):
            @pl.when(ok)
            def _(way=way):
                if wait:
                    x_copy(sec, grp, case, way).wait_recv()
                packs = {c: zero8 for c in comps}
                outer, beside = ((0, 1), (NX - 1, NX - 2))[way]
                slopes = {x: row_of(case, SLOPE, x) for x in (outer, beside)}
                couples = {x: row_of(case, COUPLE, x) for x in (outer, beside)}
                for zt in range(ZT):
                    zs = Z0 + 8 * zt
                    h1, h2 = {}, {}
                    for c in sorted(set(comps) | ({1} if 0 in comps else set()) | ({0} if 1 in comps else set())):
                        first, second = ((1, 0), (0, 1))[way]
                        h1[c] = halo[sec, way, case, c, first, 8 * zt:8 * zt + 8, :]
                        h2[c] = halo[sec, way, case, c, second, 8 * zt:8 * zt + 8, :]
                    for x in (outer, beside):
                        carry = slopes[x] * heights[zt]
                        for c in comps:
                            mate = {0: 1, 1: 0}.get(c)
                            if x == outer:
                                lap = 16.0 * h1[c] - h2[c]
                                grad = lambda k: (h2[k] - 8.0 * h1[k]) if way == 0 else (8.0 * h1[k] - h2[k])
                            else:
                                lap = -h1[c]
                                grad = lambda k: h1[k] if way == 0 else -h1[k]
                            delta = row_of(case, AROW[c], x) * lap + carry * grad(c)
                            if mate is not None:
                                delta = delta + couples[x] * grad(mate)
                            new_buf[c, case, x + 2, zs:zs + 8, :] = new_buf[c, case, x + 2, zs:zs + 8, :] + delta
                            if sec == 0:
                                packs[c] = packed(packs[c], delta, x * ZT + zt)
                if sec == 0:
                    for c in comps:
                        ysend[1, c, case] = ysend[1, c, case] + packs[c]

    def middle(sec, case, comps):
        added = rims(sec, case, comps)

        def body(x, _):
            add_rims(sec, case, added, x)
            return 0

        lax.fori_loop(2, NX - 2, body, 0)

    for copy in loads + src_loads:
        copy.wait()
    for case in range(CASES):
        inner(0, case, (0, 1, 2))
    for case in range(CASES):
        inner(0, case, (3,))
    pl.semaphore_wait(barrier, plane_n - 1 + ZRING - 1 + 2)
    for case in range(CASES):
        y_start(0, 0, case)
        x_start(0, 0, case)
    for case in range(CASES):
        y_wait(0, 0, case)
        edges(0, 0, case, (0, 1, 2))
        y_start(1, 0, case)
        x_start(1, 0, case)
    for case in range(CASES):
        y_start(0, 1, case)
        x_start(0, 1, case)

    for case in range(CASES):
        middle(0, case, (0, 1, 2))
    sent(x_copy, 0, 0, (has_up, has_down))
    for case in range(CASES):
        inner(1, case, (0, 1))

    def mean_row(case, x):
        total = s0[0, case, x + 2, Z0:Z0 + 8, :]
        for zt in range(1, ZT):
            total = total + s0[0, case, x + 2, Z0 + 8 * zt:Z0 + 8 * zt + 8, :]
        mean[x + 2, case:case + 1, :] = jnp.sum(total, axis=0, keepdims=True)

    for case in range(CASES):
        y_wait(1, 0, case)
        edges(1, 0, case, (0,))
        for x in (0, 1, NX - 2, NX - 1):
            mean_row(case, x)

    def m_copy(way):
        a, b, peer = ((NX, 0, up), (2, NX + 2, down))[way]
        return pltpu.make_async_remote_copy(
            src_ref=mean.at[pl.ds(a, 2)], dst_ref=mean.at[pl.ds(b, 2)],
            send_sem=msend_sem.at[way], recv_sem=mrecv_sem.at[way],
            device_id=peer, device_id_type=MESH)

    for way, ok in ((0, has_up), (1, has_down)):
        @pl.when(ok)
        def _(way=way):
            m_copy(way).start()

    def store_out(c):
        return [
            pltpu.make_async_copy(
                s0.at[c, :, 2 + x, pl.ds(Z0, NZ), :], out.at[c, :, :, x, :], out_sem.at[c, x])
            for x in range(NX)
        ]

    for case in range(CASES):
        middle(1, case, (0,))

        def means(x, _, case=case):
            mean_row(case, x)
            return 0

        lax.fori_loop(2, NX - 2, means, 0)
        edges(1, 0, case, (1,), wait=False)
        middle(1, case, (1,))

        def bends(x, _, case=case):
            bend = None
            for zt in range(ZT):
                zs = Z0 + 8 * zt
                f = s0[1, case, x + 2, zs:zs + 8, :]
                term = f * (s0[1, case, x + 2, zs + 1:zs + 9, :] - 2.0 * f + s0[1, case, x + 2, zs - 1:zs + 7, :])
                bend = term if bend is None else bend + term
            curv[case, pl.ds(x, 1), :] = jnp.sum(bend, axis=0, keepdims=True)
            return 0

        lax.fori_loop(0, NX, bends, 0)
    for way, ok in ((0, has_down), (1, has_up)):
        @pl.when(ok)
        def _(way=way):
            m_copy(way).wait_recv()

    grad = jnp.zeros((NX, NY), jnp.float32)
    for case in range(CASES):
        theta = THETA_STEP * temp[case].astype(jnp.float32)
        visc = jnp.exp(VISCOSITY_PRESS * pressure[case] - VISCOSITY_TEMP * theta)
        density = 1.0 - 0.6 * cavity[case].astype(jnp.float32)

        def rows(dx):
            return mean[2 + dx:2 + dx + NX, case, :]

        slope = (8.0 * (rows(1) - rows(-1)) - (rows(2) - rows(-2))) / (12.0 * NZ)
        grad = grad + (density * thick / 2.0 * slope
                       - 8.0 * visc / (thick * thick * thick) * (curv[case] / NZ))
    wall[...] = grad
    mine[0] = jnp.sum(grad * grad, axis=0, keepdims=True)

    def plane_copy(o):
        return pltpu.make_async_remote_copy(
            src_ref=mine.at[0], dst_ref=plane.at[o], send_sem=rsend_sem.at[0], recv_sem=rrecv_sem.at[0],
            device_id=plane_peer(o), device_id_type=MESH)

    def ring_copy(o):
        return pltpu.make_async_remote_copy(
            src_ref=mine2.at[0], dst_ref=ring.at[o], send_sem=rsend_sem.at[1], recv_sem=rrecv_sem.at[1],
            device_id=ring_peer(o), device_id_type=MESH)

    for o in range(1, plane_n):
        plane_copy(o).start()

    for case in range(CASES):
        y_wait(0, 1, case)
        edges(0, 1, case, (3,))
        y_start(1, 1, case)
        x_start(1, 1, case)
    for c in (0, 1):
        for copy in store_out(c):
            copy.start()
    for case in range(CASES):
        middle(0, case, (3,))
    sent(x_copy, 0, 1, (has_up, has_down))
    pltpu.make_async_copy(plane.at[pl.ds(1, plane_n - 1)], plane.at[pl.ds(1, plane_n - 1)], rrecv_sem.at[0]).wait()
    mine2[0] = mine[0] + jnp.sum(plane[1:plane_n], axis=0)
    for o in range(1, ZRING):
        ring_copy(o).start()
    for case in range(CASES):
        inner(1, case, (2, 3))
    for case in range(CASES):
        y_wait(1, 1, case)
        edges(1, 1, case, (2, 3))
        middle(1, case, (2, 3))
    for c in (2, 3):
        for copy in store_out(c):
            copy.start()
    pltpu.make_async_copy(ring.at[pl.ds(1, ZRING - 1)], ring.at[pl.ds(1, ZRING - 1)], rrecv_sem.at[1]).wait()
    total = jnp.sum(mine2[0] + jnp.sum(ring[1:ZRING], axis=0), axis=1, keepdims=True)
    wall[...] = wall[...] / jnp.sqrt(total / cells + 1e-06)

    pltpu.make_async_copy(plane.at[pl.ds(1, plane_n - 1)], plane.at[pl.ds(1, plane_n - 1)], rsend_sem.at[0]).wait()
    pltpu.make_async_copy(ring.at[pl.ds(1, ZRING - 1)], ring.at[pl.ds(1, ZRING - 1)], rsend_sem.at[1]).wait()
    for way, ok in ((0, has_up), (1, has_down)):
        @pl.when(ok)
        def _(way=way):
            m_copy(way).wait_send()
    for grp in range(2):
        sent(x_copy, 1, grp, (has_up, has_down))
        for sec in range(2):
            sent(y_copy, sec, grp, (has_right, has_left))
    for c in range(NC):
        for copy in store_out(c):
            copy.wait()


def on_device(adjoint, source, pressure, film, cavity, temp_index):
    vmem = pl.BlockSpec(memory_space=pltpu.VMEM)
    hbm = pl.BlockSpec(memory_space=pltpu.HBM)
    f32 = jnp.float32
    dma = pltpu.SemaphoreType.DMA
    given = [
        pltpu.with_memory_space_constraint(a, pltpu.HBM)
        for a in (adjoint, source, pressure, film, cavity, temp_index)
    ]
    return pl.pallas_call(
        kernel,
        out_shape=(pltpu.VMEM(adjoint.shape, f32), pltpu.VMEM(film.shape, f32)),
        in_specs=[hbm] * 6,
        out_specs=(vmem, vmem),
        scratch_shapes=[
            pltpu.VMEM(pressure.shape, f32),
            pltpu.VMEM(film.shape, f32),
            pltpu.VMEM(cavity.shape, jnp.int32),
            pltpu.SMEM(temp_index.shape, jnp.int32),
            pltpu.VMEM((NC, CASES, NX + 4, ZROWS, NY), f32),
            pltpu.VMEM((NC, CASES, NX + 4, ZROWS, NY), f32),
            pltpu.VMEM((2, 2, CASES, NC, 2, NZ, NY), f32),
            pltpu.VMEM((NC, CASES, NX, NZ, NY), f32),
            pltpu.VMEM((CASES, 13, NX, NY), f32),
            pltpu.VMEM((CASES, 4, 8, NY), f32),
            pltpu.VMEM((2, NC, CASES, 8, NY), f32),
            pltpu.VMEM((2, NC, CASES, 8, NY), f32),
            pltpu.VMEM((2, NC, CASES, 8, NY), f32),
            pltpu.VMEM((NX + 4, CASES, NY), f32),
            pltpu.VMEM((CASES, NX, NY), f32),
            pltpu.VMEM((1, 1, NY), f32),
            pltpu.VMEM((32, 1, NY), f32),
            pltpu.VMEM((1, 1, NY), f32),
            pltpu.VMEM((ZRING, 1, NY), f32),
            dma((4,)),
            dma((NX,)),
            dma((NX,)),
            dma((NC, NX)),
            dma((2, 2, CASES, 2)),
            dma((2, 2, CASES, 2)),
            dma((2, 2, CASES, 2)),
            dma((2, 2, CASES, 2)),
            dma((2,)),
            dma((2,)),
            dma((2,)),
            dma((2,)),
        ],
        compiler_params=pltpu.CompilerParams(
            collective_id=0, has_side_effects=True, vmem_limit_bytes=48 * 1024 * 1024
        ),
        name="lubrication_adjoint",
    )(*given)


def solution(mesh):
    placed = (
        P(None, None, None, "roll", "trans"),
        P(None, None, None, "roll", "trans"),
        P(None, "roll", "trans"),
        P("roll", "trans"),
        P(None, "roll", "trans"),
        P(),
    )
    return jax.shard_map(
        on_device,
        mesh=mesh,
        in_specs=placed,
        out_specs=(P(None, None, None, "roll", "trans"), P("roll", "trans")),
        check_vma=False,
    )
```

```python
import jax
import jax.numpy as jnp
from jax import lax
from jax.experimental import pallas as pl
from jax.experimental.pallas import tpu as pltpu
from jax.sharding import PartitionSpec as P

VISCOSITY_PRESS = 0.3
VISCOSITY_TEMP = 0.5
THETA_STEP = 0.2
SOUND = 0.5
KAPPA = 0.6
HEATING = 0.3
COURANT = 0.8

MESH = pl.DeviceIdType.MESH
NC = 4
CASES = 2
NZ = 32
NX = 8
NY = 128
Z0 = 8
ZROWS = 48
ZT = NZ // 8
ZRING = 8
XGROUPS = (((0, 3), (3, 1)), ((0, 2), (2, 1), (3, 1)))
YGROUPS = (((0, 3), (3, 1)), ((0, 3), (3, 1)))

STEP, SLOPE, COUPLE, HEAT, A0, A1, A3, B0, B1, B3, C0, C1, C3 = range(13)
AROW = (A0, A1, A1, A3)
BROW = (B0, B1, B1, B3)
CROW = (C0, C1, C1, C3)


def kernel(
    adjoint, source, pressure_in, film_in, cavity_in, temp_in, out, wall,
    pressure, film, cavity, temp,
    s0, s1, halo, src, coef, pcoef, ysend, yleft, yright, mean, curv, mine, plane, mine2, ring,
    small_sem, in_sem, out_sem, xsend_sem, xrecv_sem, ysend_sem, yrecv_sem,
    msend_sem, mrecv_sem, rsend_sem, rrecv_sem,
):
    nr, nt = lax.axis_size("roll"), lax.axis_size("trans")
    r, t = lax.axis_index("roll"), lax.axis_index("trans")
    core = lax.rem(r, 2)
    z = lax.rem(r // 2, ZRING)
    g = r // (2 * ZRING)
    groups = nr // (2 * ZRING)
    plane_n = groups * 2 * nt
    cells = nr * NX * nt * NY

    def plane_peer(o):
        dt, dg, dc = o // (2 * groups), (o // 2) % groups, o % 2
        row = (lax.rem(g + dg, groups) * ZRING + z) * 2 + lax.rem(core + dc, 2)
        return (row, lax.rem(t + dt, nt))

    def ring_peer(o):
        return ((g * ZRING + lax.rem(z + o, ZRING)) * 2 + core, t)

    up = (lax.rem(r + 1, nr), t)
    down = (lax.rem(r + nr - 1, nr), t)
    right = (r, lax.rem(t + 1, nt))
    left = (r, lax.rem(t + nt - 1, nt))
    has_up, has_down = r < nr - 1, r > 0
    has_right, has_left = t < nt - 1, t > 0

    barrier = pltpu.get_barrier_semaphore()
    for o in range(1, plane_n):
        pl.semaphore_signal(barrier, inc=1, device_id=plane_peer(o), device_id_type=MESH)
    for o in range(1, ZRING):
        pl.semaphore_signal(barrier, inc=1, device_id=ring_peer(o), device_id_type=MESH)
    for peer in (up, down):
        pl.semaphore_signal(barrier, inc=1, device_id=peer, device_id_type=MESH)

    smalls = [
        pltpu.make_async_copy(given, held, small_sem.at[k])
        for k, (given, held) in enumerate(
            ((pressure_in, pressure), (film_in, film), (cavity_in, cavity), (temp_in, temp)))
    ]
    loads = [
        pltpu.make_async_copy(
            adjoint.at[:, :, :, x, :], s0.at[:, :, 2 + x, pl.ds(Z0, NZ), :], in_sem.at[0])
        for x in range(NX)
    ]
    src_loads = [
        pltpu.make_async_copy(source.at[:, :, :, x, :], src.at[:, :, x], in_sem.at[1])
        for x in range(NX)
    ]
    for copy in smalls + loads + src_loads:
        copy.start()

    lane = lax.broadcasted_iota(jnp.int32, (8, NY), 1)
    sub = lax.broadcasted_iota(jnp.int32, (8, NY), 0)
    lane4, lane_in4 = lane // 4, lane % 4
    lo_half = lane_in4 < 2
    near1, near2 = lane_in4 == 1, lane_in4 == 2
    rim = jnp.logical_or(lane < 2, lane >= NY - 2)
    heights = [(sub.astype(jnp.float32) + (8 * zt + 0.5)) / NZ for zt in range(ZT)]
    zero8 = jnp.zeros((8, NY), jnp.float32)

    for buf in (s0, s1):
        def clear(i, _, buf=buf):
            for case in range(CASES):
                for c in range(NC):
                    buf[c, case, i, 0:Z0, :] = zero8
                    buf[c, case, i, Z0 + NZ:ZROWS, :] = zero8
            return 0
        lax.fori_loop(0, NX + 4, clear, 0)

        def clear_row(i, _, buf=buf):
            for case in range(CASES):
                for x in (0, 1, NX + 2, NX + 3):
                    for zt in range(ZT):
                        buf[i, case, x, Z0 + 8 * zt:Z0 + 8 * zt + 8, :] = zero8
            return 0
        lax.fori_loop(0, NC, clear_row, 0)

    def clear_pack(i, _):
        for case in range(CASES):
            ysend[1, i, case] = zero8
        return 0
    lax.fori_loop(0, NC, clear_pack, 0)

    @pl.when(jnp.logical_not(has_down))
    def _():
        mean[0:2] = jnp.zeros((2, CASES, NY), jnp.float32)

    @pl.when(jnp.logical_not(has_up))
    def _():
        mean[NX + 2:NX + 4] = jnp.zeros((2, CASES, NY), jnp.float32)

    @pl.when(jnp.logical_not(has_left))
    def _():
        yleft[...] = jnp.zeros(yleft.shape, jnp.float32)

    @pl.when(jnp.logical_not(has_right))
    def _():
        yright[...] = jnp.zeros(yright.shape, jnp.float32)

    for copy in smalls:
        copy.wait()
    thick = film[...]
    for case in range(CASES):
        theta = THETA_STEP * temp[case].astype(jnp.float32)
        visc = jnp.exp(VISCOSITY_PRESS * pressure[case] - VISCOSITY_TEMP * theta)
        fcoef = 4.0 * visc / (thick * thick)
        density = 1.0 - 0.6 * cavity[case].astype(jnp.float32)
        step = COURANT / (32.0 / 3.0 * visc + 4.0 * fcoef + 2.0 * SOUND + 1.0)
        sv, sf = step * visc, step * fcoef
        table = {
            STEP: step, SLOPE: step * density / 12.0, COUPLE: step * (SOUND / 12.0), HEAT: HEATING * sv,
        }
        for scale, a, b, c in ((0.5, A0, B0, C0), (1.0, A1, B1, C1), (KAPPA, A3, B3, C3)):
            table[a] = (scale / 12.0) * sv
            table[b] = scale * sf
            table[c] = 1.0 - scale * (5.0 * sv + 2.0 * sf)
        for k, value in table.items():
            coef[case, k] = value
        for k, value in ((0, sv), (1, step)):
            acc = zero8
            for x in range(NX):
                here = jnp.logical_and(lane4 == ZT * x, sub == x)
                acc = jnp.where(here, pltpu.roll(value, 4 * ZT * x + 2, 1), acc)
            acc = acc + pltpu.roll(acc, 4, 1)
            acc = acc + pltpu.roll(acc, 8, 1)
            spread = jnp.broadcast_to(jnp.sum(acc, axis=0, keepdims=True), (8, NY))
            if k == 0:
                pcoef[case, 0] = (0.5 / 12.0) * spread
                pcoef[case, 1] = (1.0 / 12.0) * spread
                pcoef[case, 2] = (KAPPA / 12.0) * spread
            else:
                pcoef[case, 3] = (SOUND / 12.0) * spread

    def x_copy(sec, grp, case, way):
        buf = (s0, s1)[sec]
        c, n = XGROUPS[sec][grp]
        a, peer = ((NX, up), (2, down))[way]
        return pltpu.make_async_remote_copy(
            src_ref=buf.at[pl.ds(c, n), case, pl.ds(a, 2), pl.ds(Z0, NZ), :],
            dst_ref=halo.at[sec, way, case, pl.ds(c, n)],
            send_sem=xsend_sem.at[sec, grp, way],
            recv_sem=xrecv_sem.at[sec, grp, case, way],
            device_id=peer, device_id_type=MESH)

    def y_copy(sec, grp, case, way):
        c, n = YGROUPS[sec][grp]
        dst, peer = ((yleft, right), (yright, left))[way]
        return pltpu.make_async_remote_copy(
            src_ref=ysend.at[sec, pl.ds(c, n), case],
            dst_ref=dst.at[sec, pl.ds(c, n), case],
            send_sem=ysend_sem.at[sec, way],
            recv_sem=yrecv_sem.at[sec, grp, case, way],
            device_id=peer, device_id_type=MESH)

    def x_start(sec, grp, case):
        for way, ok in ((0, has_up), (1, has_down)):
            @pl.when(ok)
            def _(way=way):
                x_copy(sec, grp, case, way).start()

    def y_start(sec, grp, case):
        for way, ok in ((0, has_right), (1, has_left)):
            @pl.when(ok)
            def _(way=way):
                y_copy(sec, grp, case, way).start()

    def y_wait(sec, grp, case):
        for way, ok in ((0, has_left), (1, has_right)):
            @pl.when(ok)
            def _(way=way):
                y_copy(sec, grp, case, way).wait_recv()

    def x_sent(sec, grp):
        c, n = XGROUPS[sec][grp]
        for way, ok in ((0, has_up), (1, has_down)):
            @pl.when(ok)
            def _(way=way):
                both = halo.at[sec, way, :, pl.ds(c, n)]
                pltpu.make_async_copy(both, both, xsend_sem.at[sec, grp, way]).wait()

    def y_sent(sec):
        for way, ok in ((0, has_right), (1, has_left)):
            @pl.when(ok)
            def _(way=way):
                pltpu.make_async_copy(ysend.at[sec], ysend.at[sec], ysend_sem.at[sec, way]).wait()

    def row_of(case, k, x):
        return jnp.broadcast_to(coef[case, k, pl.ds(x, 1), :], (8, NY))

    def packed(acc, tile, q):
        return jnp.where(lane4 == q, pltpu.roll(tile, 4 * q + 2, 1), acc)

    def inner(sec, case, comps):
        cur, new_buf = ((s0, s1), (s1, s0))[sec]
        need_x = sorted(set(comps) | ({1} if 0 in comps else set()) | ({0} if 1 in comps else set()))
        need_y = sorted(set(comps) | ({2} if 0 in comps else set()) | ({0} if 2 in comps else set()))

        def body(x, _):
            def row(k):
                return row_of(case, k, x)

            step, slope, couple = row(STEP), row(SLOPE), row(COUPLE)
            packs = {}
            if sec == 0:
                packs = {c: ysend[1, c, case] for c in comps}
            for zt in range(ZT):
                zs = Z0 + 8 * zt
                q = x * ZT + zt
                carry = slope * heights[zt]

                def at(c, dx=0, dz=0):
                    return cur[c, case, x + 2 + dx, zs + dz:zs + dz + 8, :]

                xd, yd, e1, e2 = {}, {}, {}, {}
                for c in need_y:
                    f = at(c)
                    p1, m1 = pltpu.roll(f, NY - 1, 1), pltpu.roll(f, 1, 1)
                    p2, m2 = pltpu.roll(f, NY - 2, 1), pltpu.roll(f, 2, 1)
                    if (c == 2 and 0 in comps) or (c == 0 and 2 in comps):
                        yd[c] = 8.0 * (p1 - m1) - (p2 - m2)
                    e1[c], e2[c] = p1 + m1, p2 + m2
                for c in need_x:
                    p1, m1, p2, m2 = at(c, 1), at(c, -1), at(c, 2), at(c, -2)
                    xd[c] = 8.0 * (p1 - m1) - (p2 - m2)
                    if c in comps:
                        e1[c], e2[c] = e1[c] + (p1 + m1), e2[c] + (p2 + m2)
                for c in comps:
                    new = row(CROW[c]) * at(c) + row(AROW[c]) * (16.0 * e1[c] - e2[c])
                    new = new + row(BROW[c]) * (at(c, 0, 1) + at(c, 0, -1))
                    new = new + (carry * xd[c] + step * src[c, case, x, 8 * zt:8 * zt + 8, :])
                    if c == 0:
                        new = new + couple * (xd[1] + yd[2])
                    elif c == 1:
                        new = new + couple * xd[0]
                    elif c == 2:
                        new = new + couple * yd[0]
                    else:
                        new = new + row(HEAT) * at(1)
                    new_buf[c, case, x + 2, zs:zs + 8, :] = new
                    if sec == 0:
                        packs[c] = packed(packs[c], new, q)
            for c, value in packs.items():
                ysend[1, c, case] = value
            return 0

        lax.fori_loop(0, NX, body, 0, unroll=2)

    def rims(sec, case, comps):
        near, far, cross = {}, {}, {}
        for c in sorted(set(comps) | ({2} if 0 in comps else set()) | ({0} if 2 in comps else set())):
            d = jnp.where(lo_half, yleft[sec, c, case], yright[sec, c, case]) - ysend[sec, c, case]
            p1, m1 = pltpu.roll(d, NY - 1, 1), pltpu.roll(d, 1, 1)
            far_d = jnp.where(lo_half, pltpu.roll(d, NY - 2, 1), pltpu.roll(d, 2, 1))
            near[c] = 16.0 * jnp.where(near1, p1, jnp.where(near2, m1, 0.0)) - far_d
            cross[c] = 8.0 * jnp.where(near1, p1, jnp.where(near2, -m1, 0.0)) + jnp.where(lo_half, -far_d, far_d)
        result = {}
        for c in comps:
            value = pcoef[case, (0, 1, 1, 2)[c]] * near[c]
            if c in (0, 2):
                value = value + pcoef[case, 3] * cross[2 - c]
            result[c] = value
        return result

    def add_rims(sec, case, added, x):
        new_buf = (s1, s0)[sec]
        for c, value in added.items():
            for zt in range(ZT):
                zs = Z0 + 8 * zt
                here = jnp.where(rim, pltpu.roll(value, NY - 2 - 4 * (x * ZT + zt), 1), 0.0)
                new_buf[c, case, x + 2, zs:zs + 8, :] = new_buf[c, case, x + 2, zs:zs + 8, :] + here

    def edges(sec, grps, case, comps):
        new_buf = (s1, s0)[sec]
        added = rims(sec, case, comps)
        for x in (0, 1, NX - 2, NX - 1):
            add_rims(sec, case, added, x)
        if sec == 0:
            for c in comps:
                ysend[1, c, case] = ysend[1, c, case] + added[c]
        for way, ok in ((0, has_down), (1, has_up)):
            @pl.when(ok)
            def _(way=way):
                for grp in grps:
                    x_copy(sec, grp, case, way).wait_recv()
                packs = {c: zero8 for c in comps}
                outer, beside = ((0, 1), (NX - 1, NX - 2))[way]
                slopes = {x: row_of(case, SLOPE, x) for x in (outer, beside)}
                couples = {x: row_of(case, COUPLE, x) for x in (outer, beside)}
                for zt in range(ZT):
                    zs = Z0 + 8 * zt
                    h1, h2 = {}, {}
                    for c in sorted(set(comps) | ({1} if 0 in comps else set()) | ({0} if 1 in comps else set())):
                        first, second = ((1, 0), (0, 1))[way]
                        h1[c] = halo[sec, way, case, c, first, 8 * zt:8 * zt + 8, :]
                        h2[c] = halo[sec, way, case, c, second, 8 * zt:8 * zt + 8, :]
                    for x in (outer, beside):
                        carry = slopes[x] * heights[zt]
                        for c in comps:
                            mate = {0: 1, 1: 0}.get(c)
                            if x == outer:
                                lap = 16.0 * h1[c] - h2[c]
                                grad = lambda k: (h2[k] - 8.0 * h1[k]) if way == 0 else (8.0 * h1[k] - h2[k])
                            else:
                                lap = -h1[c]
                                grad = lambda k: h1[k] if way == 0 else -h1[k]
                            delta = row_of(case, AROW[c], x) * lap + carry * grad(c)
                            if mate is not None:
                                delta = delta + couples[x] * grad(mate)
                            new_buf[c, case, x + 2, zs:zs + 8, :] = new_buf[c, case, x + 2, zs:zs + 8, :] + delta
                            if sec == 0:
                                packs[c] = packed(packs[c], delta, x * ZT + zt)
                if sec == 0:
                    for c in comps:
                        ysend[1, c, case] = ysend[1, c, case] + packs[c]

    def middle(sec, case, comps):
        added = rims(sec, case, comps)

        def body(x, _):
            add_rims(sec, case, added, x)
            return 0

        lax.fori_loop(2, NX - 2, body, 0)

    pltpu.make_async_copy(adjoint, adjoint, in_sem.at[0]).wait()
    for case in range(CASES):
        def pack_rows(x, accs, case=case):
            accs = list(accs)
            for c in range(NC):
                for zt in range(ZT):
                    accs[c] = packed(accs[c], s0[c, case, x + 2, Z0 + 8 * zt:Z0 + 8 * zt + 8, :], x * ZT + zt)
            return tuple(accs)

        accs = lax.fori_loop(0, NX, pack_rows, (zero8,) * NC)
        for c in range(NC):
            ysend[0, c, case] = accs[c]
    pl.semaphore_wait(barrier, plane_n - 1 + ZRING - 1 + 2)
    for case in range(CASES):
        x_start(0, 0, case)
        y_start(0, 0, case)
    pltpu.make_async_copy(source, source, in_sem.at[1]).wait()
    for case in range(CASES):
        inner(0, case, (0, 1, 2))
    for case in range(CASES):
        y_wait(0, 0, case)
        edges(0, (0,), case, (0, 1, 2))
        y_start(1, 0, case)
        x_start(1, 0, case)
    for case in range(CASES):
        y_start(0, 1, case)
        x_start(0, 1, case)
        x_start(1, 1, case)

    for case in range(CASES):
        middle(0, case, (0, 1, 2))
    x_sent(0, 0)
    for case in range(CASES):
        inner(0, case, (3,))
    for case in range(CASES):
        inner(1, case, (0, 1))

    def mean_row(case, x):
        total = s0[0, case, x + 2, Z0:Z0 + 8, :]
        for zt in range(1, ZT):
            total = total + s0[0, case, x + 2, Z0 + 8 * zt:Z0 + 8 * zt + 8, :]
        mean[x + 2, case:case + 1, :] = jnp.sum(total, axis=0, keepdims=True)

    for case in range(CASES):
        y_wait(1, 0, case)
        edges(1, (0,), case, (0,))
        for x in (0, 1, NX - 2, NX - 1):
            mean_row(case, x)

    def m_copy(way):
        a, b, peer = ((NX, 0, up), (2, NX + 2, down))[way]
        return pltpu.make_async_remote_copy(
            src_ref=mean.at[pl.ds(a, 2)], dst_ref=mean.at[pl.ds(b, 2)],
            send_sem=msend_sem.at[way], recv_sem=mrecv_sem.at[way],
            device_id=peer, device_id_type=MESH)

    for way, ok in ((0, has_up), (1, has_down)):
        @pl.when(ok)
        def _(way=way):
            m_copy(way).start()

    for case in range(CASES):
        y_wait(0, 1, case)
        edges(0, (1,), case, (3,))
        y_start(1, 1, case)
        x_start(1, 2, case)

    def store_out(c):
        return [
            pltpu.make_async_copy(
                s0.at[c, :, 2 + x, pl.ds(Z0, NZ), :], out.at[c, :, :, x, :], out_sem.at[c])
            for x in range(NX)
        ]

    for case in range(CASES):
        middle(1, case, (0,))

        def means(x, _, case=case):
            mean_row(case, x)
            return 0

        lax.fori_loop(2, NX - 2, means, 0)
        edges(1, (), case, (1,))
        middle(1, case, (1,))

        def bends(x, _, case=case):
            bend = None
            for zt in range(ZT):
                zs = Z0 + 8 * zt
                f = s0[1, case, x + 2, zs:zs + 8, :]
                term = f * (s0[1, case, x + 2, zs + 1:zs + 9, :] - 2.0 * f + s0[1, case, x + 2, zs - 1:zs + 7, :])
                bend = term if bend is None else bend + term
            curv[case, pl.ds(x, 1), :] = jnp.sum(bend, axis=0, keepdims=True)
            return 0

        lax.fori_loop(0, NX, bends, 0)
    for way, ok in ((0, has_down), (1, has_up)):
        @pl.when(ok)
        def _(way=way):
            m_copy(way).wait_recv()

    grad = jnp.zeros((NX, NY), jnp.float32)
    for case in range(CASES):
        theta = THETA_STEP * temp[case].astype(jnp.float32)
        visc = jnp.exp(VISCOSITY_PRESS * pressure[case] - VISCOSITY_TEMP * theta)
        density = 1.0 - 0.6 * cavity[case].astype(jnp.float32)

        def rows(dx):
            return mean[2 + dx:2 + dx + NX, case, :]

        slope = (8.0 * (rows(1) - rows(-1)) - (rows(2) - rows(-2))) / (12.0 * NZ)
        grad = grad + (density * thick / 2.0 * slope
                       - 8.0 * visc / (thick * thick * thick) * (curv[case] / NZ))
    wall[...] = grad
    mine[0] = jnp.sum(grad * grad, axis=0, keepdims=True)

    def plane_copy(o):
        return pltpu.make_async_remote_copy(
            src_ref=mine.at[0], dst_ref=plane.at[o], send_sem=rsend_sem.at[0], recv_sem=rrecv_sem.at[0],
            device_id=plane_peer(o), device_id_type=MESH)

    def ring_copy(o):
        return pltpu.make_async_remote_copy(
            src_ref=mine2.at[0], dst_ref=ring.at[o], send_sem=rsend_sem.at[1], recv_sem=rrecv_sem.at[1],
            device_id=ring_peer(o), device_id_type=MESH)

    def hops(o):
        dt = o // (2 * groups)
        return min(dt % 4, 4 - dt % 4) + 2 * (dt >= 4) + (o // 2) % groups

    for o in sorted(range(1, plane_n), key=lambda o: -hops(o)):
        plane_copy(o).start()

    for c in (0, 1):
        for copy in store_out(c):
            copy.start()
    for case in range(CASES):
        middle(0, case, (3,))
    x_sent(0, 1)
    for case in range(CASES):
        inner(1, case, (2, 3))
    pltpu.make_async_copy(plane.at[pl.ds(1, plane_n - 1)], plane.at[pl.ds(1, plane_n - 1)], rrecv_sem.at[0]).wait()
    mine2[0] = mine[0] + jnp.sum(plane[1:plane_n], axis=0)
    for o in sorted(range(1, ZRING), key=lambda o: -min(o, ZRING - o)):
        ring_copy(o).start()
    for case in range(CASES):
        y_wait(1, 1, case)
        edges(1, (1, 2), case, (2, 3))
        middle(1, case, (2, 3))
    for c in (2, 3):
        for copy in store_out(c):
            copy.start()
    pltpu.make_async_copy(ring.at[pl.ds(1, ZRING - 1)], ring.at[pl.ds(1, ZRING - 1)], rrecv_sem.at[1]).wait()
    total = jnp.sum(mine2[0] + jnp.sum(ring[1:ZRING], axis=0), axis=1, keepdims=True)
    wall[...] = wall[...] / jnp.sqrt(total / cells + 1e-06)

    pltpu.make_async_copy(plane.at[pl.ds(1, plane_n - 1)], plane.at[pl.ds(1, plane_n - 1)], rsend_sem.at[0]).wait()
    pltpu.make_async_copy(ring.at[pl.ds(1, ZRING - 1)], ring.at[pl.ds(1, ZRING - 1)], rsend_sem.at[1]).wait()
    for way, ok in ((0, has_up), (1, has_down)):
        @pl.when(ok)
        def _(way=way):
            m_copy(way).wait_send()
    for grp in range(3):
        x_sent(1, grp)
    for sec in range(2):
        y_sent(sec)
    for c in range(NC):
        pltpu.make_async_copy(out.at[c], out.at[c], out_sem.at[c]).wait()


def on_device(adjoint, source, pressure, film, cavity, temp_index):
    vmem = pl.BlockSpec(memory_space=pltpu.VMEM)
    hbm = pl.BlockSpec(memory_space=pltpu.HBM)
    f32 = jnp.float32
    dma = pltpu.SemaphoreType.DMA
    given = [
        pltpu.with_memory_space_constraint(a, pltpu.HBM)
        for a in (adjoint, source, pressure, film, cavity, temp_index)
    ]
    return pl.pallas_call(
        kernel,
        out_shape=(pltpu.VMEM(adjoint.shape, f32), pltpu.VMEM(film.shape, f32)),
        in_specs=[hbm] * 6,
        out_specs=(vmem, vmem),
        scratch_shapes=[
            pltpu.VMEM(pressure.shape, f32),
            pltpu.VMEM(film.shape, f32),
            pltpu.VMEM(cavity.shape, jnp.int32),
            pltpu.SMEM(temp_index.shape, jnp.int32),
            pltpu.VMEM((NC, CASES, NX + 4, ZROWS, NY), f32),
            pltpu.VMEM((NC, CASES, NX + 4, ZROWS, NY), f32),
            pltpu.VMEM((2, 2, CASES, NC, 2, NZ, NY), f32),
            pltpu.VMEM((NC, CASES, NX, NZ, NY), f32),
            pltpu.VMEM((CASES, 13, NX, NY), f32),
            pltpu.VMEM((CASES, 4, 8, NY), f32),
            pltpu.VMEM((2, NC, CASES, 8, NY), f32),
            pltpu.VMEM((2, NC, CASES, 8, NY), f32),
            pltpu.VMEM((2, NC, CASES, 8, NY), f32),
            pltpu.VMEM((NX + 4, CASES, NY), f32),
            pltpu.VMEM((CASES, NX, NY), f32),
            pltpu.VMEM((1, 1, NY), f32),
            pltpu.VMEM((32, 1, NY), f32),
            pltpu.VMEM((1, 1, NY), f32),
            pltpu.VMEM((ZRING, 1, NY), f32),
            dma((4,)),
            dma((2,)),
            dma((NC,)),
            dma((2, 3, 2)),
            dma((2, 3, CASES, 2)),
            dma((2, 2)),
            dma((2, 2, CASES, 2)),
            dma((2,)),
            dma((2,)),
            dma((2,)),
            dma((2,)),
        ],
        compiler_params=pltpu.CompilerParams(
            collective_id=0, has_side_effects=True, vmem_limit_bytes=48 * 1024 * 1024
        ),
        name="lubrication_adjoint",
    )(*given)


def solution(mesh):
    placed = (
        P(None, None, None, "roll", "trans"),
        P(None, None, None, "roll", "trans"),
        P(None, "roll", "trans"),
        P("roll", "trans"),
        P(None, "roll", "trans"),
        P(),
    )
    return jax.shard_map(
        on_device,
        mesh=mesh,
        in_specs=placed,
        out_specs=(P(None, None, None, "roll", "trans"), P("roll", "trans")),
        check_vma=False,
    )
```

```python
import jax
import jax.numpy as jnp
from jax import lax
from jax.experimental import pallas as pl
from jax.experimental.pallas import tpu as pltpu
from jax.sharding import PartitionSpec as P

VISCOSITY_PRESS = 0.3
VISCOSITY_TEMP = 0.5
THETA_STEP = 0.2
SOUND = 0.5
KAPPA = 0.6
HEATING = 0.3
COURANT = 0.8

MESH = pl.DeviceIdType.MESH
NC = 4
CASES = 2
NZ = 32
NX = 8
NY = 128
Z0 = 8
ZROWS = 48
ZT = NZ // 8
ZRING = 8
XGROUPS = (((0, 3), (3, 1)), ((0, 2), (2, 1), (3, 1)))
YGROUPS = (((0, 3), (3, 1)), ((0, 3), (3, 1)))

STEP, SLOPE, COUPLE, HEAT, A0, A1, A3, B0, B1, B3, C0, C1, C3 = range(13)
AROW = (A0, A1, A1, A3)
BROW = (B0, B1, B1, B3)
CROW = (C0, C1, C1, C3)


def kernel(
    adjoint, source, pressure_in, film_in, cavity_in, temp_in, out, wall,
    pressure, film, cavity, temp,
    s0, s1, halo, src, coef, pcoef, ysend, yleft, yright, mean, curv, zsum, zdiag, part, beside, mine, plane, mine2, ring,
    small_sem, in_sem, out_sem, xsend_sem, xrecv_sem, ysend_sem, yrecv_sem,
    msend_sem, mrecv_sem, dsend_sem, drecv_sem, rsend_sem, rrecv_sem,
):
    nr, nt = lax.axis_size("roll"), lax.axis_size("trans")
    r, t = lax.axis_index("roll"), lax.axis_index("trans")
    core = lax.rem(r, 2)
    z = lax.rem(r // 2, ZRING)
    g = r // (2 * ZRING)
    groups = nr // (2 * ZRING)
    plane_n = groups * 2 * nt
    cells = nr * NX * nt * NY

    def plane_peer(o):
        dt, dg, dc = o // (2 * groups), (o // 2) % groups, o % 2
        row = (lax.rem(g + dg, groups) * ZRING + z) * 2 + lax.rem(core + dc, 2)
        return (row, lax.rem(t + dt, nt))

    def ring_peer(o):
        return ((g * ZRING + lax.rem(z + o, ZRING)) * 2 + core, t)

    up = (lax.rem(r + 1, nr), t)
    down = (lax.rem(r + nr - 1, nr), t)
    right = (r, lax.rem(t + 1, nt))
    left = (r, lax.rem(t + nt - 1, nt))
    has_up, has_down = r < nr - 1, r > 0
    has_right, has_left = t < nt - 1, t > 0

    barrier = pltpu.get_barrier_semaphore()
    for o in range(1, plane_n):
        pl.semaphore_signal(barrier, inc=1, device_id=plane_peer(o), device_id_type=MESH)
    for o in range(1, ZRING):
        pl.semaphore_signal(barrier, inc=1, device_id=ring_peer(o), device_id_type=MESH)
    corners = [[(row[0], column[1]) for column in (right, left)] for row in (down, up)]
    for peer in [up, down] + corners[0] + corners[1]:
        pl.semaphore_signal(barrier, inc=1, device_id=peer, device_id_type=MESH)

    smalls = [
        pltpu.make_async_copy(given, held, small_sem.at[k])
        for k, (given, held) in enumerate(
            ((pressure_in, pressure), (film_in, film), (cavity_in, cavity), (temp_in, temp)))
    ]
    loads = [
        pltpu.make_async_copy(
            adjoint.at[:, :, :, x, :], s0.at[:, :, 2 + x, pl.ds(Z0, NZ), :], in_sem.at[0])
        for x in range(NX)
    ]
    src_loads = [
        pltpu.make_async_copy(source.at[:, :, :, x, :], src.at[:, :, x], in_sem.at[1])
        for x in range(NX)
    ]
    for copy in smalls + loads + src_loads:
        copy.start()

    lane = lax.broadcasted_iota(jnp.int32, (8, NY), 1)
    sub = lax.broadcasted_iota(jnp.int32, (8, NY), 0)
    lane4, lane_in4 = lane // 4, lane % 4
    lo_half = lane_in4 < 2
    near1, near2 = lane_in4 == 1, lane_in4 == 2
    rim = jnp.logical_or(lane < 2, lane >= NY - 2)
    heights = [(sub.astype(jnp.float32) + (8 * zt + 0.5)) / NZ for zt in range(ZT)]
    zero8 = jnp.zeros((8, NY), jnp.float32)

    for buf in (s0, s1):
        def clear(i, _, buf=buf):
            for case in range(CASES):
                for c in range(NC):
                    buf[c, case, i, 0:Z0, :] = zero8
                    buf[c, case, i, Z0 + NZ:ZROWS, :] = zero8
            return 0
        lax.fori_loop(0, NX + 4, clear, 0)

        def clear_row(i, _, buf=buf):
            for case in range(CASES):
                for x in (0, 1, NX + 2, NX + 3):
                    for zt in range(ZT):
                        buf[i, case, x, Z0 + 8 * zt:Z0 + 8 * zt + 8, :] = zero8
            return 0
        lax.fori_loop(0, NC, clear_row, 0)

    def clear_pack(i, _):
        for case in range(CASES):
            ysend[1, i, case] = zero8
        return 0
    lax.fori_loop(0, NC, clear_pack, 0)

    @pl.when(jnp.logical_not(has_down))
    def _():
        mean[0:2] = jnp.zeros((2, CASES, NY), jnp.float32)

    @pl.when(jnp.logical_not(has_up))
    def _():
        mean[NX + 2:NX + 4] = jnp.zeros((2, CASES, NY), jnp.float32)

    @pl.when(jnp.logical_not(has_left))
    def _():
        yleft[...] = jnp.zeros(yleft.shape, jnp.float32)
        zdiag[:, 0] = jnp.zeros((2, 2, 8, NY), jnp.float32)

    @pl.when(jnp.logical_not(has_right))
    def _():
        yright[...] = jnp.zeros(yright.shape, jnp.float32)
        zdiag[:, 1] = jnp.zeros((2, 2, 8, NY), jnp.float32)

    for copy in smalls:
        copy.wait()
    thick = film[...]
    for case in range(CASES):
        theta = THETA_STEP * temp[case].astype(jnp.float32)
        visc = jnp.exp(VISCOSITY_PRESS * pressure[case] - VISCOSITY_TEMP * theta)
        fcoef = 4.0 * visc / (thick * thick)
        density = 1.0 - 0.6 * cavity[case].astype(jnp.float32)
        step = COURANT / (32.0 / 3.0 * visc + 4.0 * fcoef + 2.0 * SOUND + 1.0)
        sv, sf = step * visc, step * fcoef
        table = {
            STEP: step, SLOPE: step * density / 12.0, COUPLE: step * (SOUND / 12.0), HEAT: HEATING * sv,
        }
        for scale, a, b, c in ((0.5, A0, B0, C0), (1.0, A1, B1, C1), (KAPPA, A3, B3, C3)):
            table[a] = (scale / 12.0) * sv
            table[b] = scale * sf
            table[c] = 1.0 - scale * (5.0 * sv + 2.0 * sf)
        for k, value in table.items():
            coef[case, k] = value
        for k, value in ((0, sv), (1, step)):
            acc = zero8
            for x in range(NX):
                here = jnp.logical_and(lane4 == ZT * x, sub == x)
                acc = jnp.where(here, pltpu.roll(value, 4 * ZT * x + 2, 1), acc)
            acc = acc + pltpu.roll(acc, 4, 1)
            acc = acc + pltpu.roll(acc, 8, 1)
            spread = jnp.broadcast_to(jnp.sum(acc, axis=0, keepdims=True), (8, NY))
            if k == 0:
                pcoef[case, 0] = (0.5 / 12.0) * spread
                pcoef[case, 1] = (1.0 / 12.0) * spread
                pcoef[case, 2] = (KAPPA / 12.0) * spread
            else:
                pcoef[case, 3] = (SOUND / 12.0) * spread

    for side in range(2):
        for k in range(4):
            zsum[side, k] = zero8
            part[side, k] = zero8
        for case in range(CASES):
            for i in range(2):
                x = (i, NX - 1 - i)[side]
                for j, k in enumerate((A0, SLOPE, COUPLE)):
                    part[side, 1 + j, 2 * case + i:2 * case + i + 1, :] = coef[case, k, x:x + 1, :]

    def x_copy(sec, grp, case, way):
        buf = (s0, s1)[sec]
        c, n = XGROUPS[sec][grp]
        a, peer = ((NX, up), (2, down))[way]
        return pltpu.make_async_remote_copy(
            src_ref=buf.at[pl.ds(c, n), case, pl.ds(a, 2), pl.ds(Z0, NZ), :],
            dst_ref=halo.at[sec, way, case, pl.ds(c, n)],
            send_sem=xsend_sem.at[sec, grp, way],
            recv_sem=xrecv_sem.at[sec, grp, case, way],
            device_id=peer, device_id_type=MESH)

    def y_copy(sec, grp, case, way):
        c, n = YGROUPS[sec][grp]
        dst, peer = ((yleft, right), (yright, left))[way]
        return pltpu.make_async_remote_copy(
            src_ref=ysend.at[sec, pl.ds(c, n), case],
            dst_ref=dst.at[sec, pl.ds(c, n), case],
            send_sem=ysend_sem.at[sec, way],
            recv_sem=yrecv_sem.at[sec, grp, case, way],
            device_id=peer, device_id_type=MESH)

    def x_start(sec, grp, case):
        for way, ok in ((0, has_up), (1, has_down)):
            @pl.when(ok)
            def _(way=way):
                x_copy(sec, grp, case, way).start()

    def y_start(sec, grp, case):
        for way, ok in ((0, has_right), (1, has_left)):
            @pl.when(ok)
            def _(way=way):
                y_copy(sec, grp, case, way).start()

    def y_wait(sec, grp, case):
        for way, ok in ((0, has_left), (1, has_right)):
            @pl.when(ok)
            def _(way=way):
                y_copy(sec, grp, case, way).wait_recv()

    def x_sent(sec, grp):
        c, n = XGROUPS[sec][grp]
        for way, ok in ((0, has_up), (1, has_down)):
            @pl.when(ok)
            def _(way=way):
                both = halo.at[sec, way, :, pl.ds(c, n)]
                pltpu.make_async_copy(both, both, xsend_sem.at[sec, grp, way]).wait()

    def y_sent(sec):
        for way, ok in ((0, has_right), (1, has_left)):
            @pl.when(ok)
            def _(way=way):
                pltpu.make_async_copy(ysend.at[sec], ysend.at[sec], ysend_sem.at[sec, way]).wait()

    def row_of(case, k, x):
        return jnp.broadcast_to(coef[case, k, pl.ds(x, 1), :], (8, NY))

    def packed(acc, tile, q):
        return jnp.where(lane4 == q, pltpu.roll(tile, 4 * q + 2, 1), acc)

    def inner(sec, case, comps, part_of=None):
        cur, new_buf = ((s0, s1), (s1, s0))[sec]
        need_x = sorted(set(comps) | ({1} if 0 in comps else set()) | ({0} if 1 in comps else set()))
        need_y = sorted(set(comps) | ({2} if 0 in comps else set()) | ({0} if 2 in comps else set()))

        def body(i, _):
            x = i + 4 * (i // 2) if part_of == 0 else i

            def row(k):
                return row_of(case, k, x)

            step, slope, couple = row(STEP), row(SLOPE), row(COUPLE)
            packs = {}
            if sec == 0:
                packs = {c: ysend[1, c, case] for c in comps}
            for zt in range(ZT):
                zs = Z0 + 8 * zt
                q = x * ZT + zt
                carry = slope * heights[zt]

                def at(c, dx=0, dz=0):
                    return cur[c, case, x + 2 + dx, zs + dz:zs + dz + 8, :]

                xd, yd, e1, e2 = {}, {}, {}, {}
                for c in need_y:
                    f = at(c)
                    p1, m1 = pltpu.roll(f, NY - 1, 1), pltpu.roll(f, 1, 1)
                    p2, m2 = pltpu.roll(f, NY - 2, 1), pltpu.roll(f, 2, 1)
                    if (c == 2 and 0 in comps) or (c == 0 and 2 in comps):
                        yd[c] = 8.0 * (p1 - m1) - (p2 - m2)
                    e1[c], e2[c] = p1 + m1, p2 + m2
                for c in need_x:
                    p1, m1, p2, m2 = at(c, 1), at(c, -1), at(c, 2), at(c, -2)
                    xd[c] = 8.0 * (p1 - m1) - (p2 - m2)
                    if c in comps:
                        e1[c], e2[c] = e1[c] + (p1 + m1), e2[c] + (p2 + m2)
                for c in comps:
                    new = row(CROW[c]) * at(c) + row(AROW[c]) * (16.0 * e1[c] - e2[c])
                    new = new + row(BROW[c]) * (at(c, 0, 1) + at(c, 0, -1))
                    new = new + (carry * xd[c] + step * src[c, case, x, 8 * zt:8 * zt + 8, :])
                    if c == 0:
                        new = new + couple * (xd[1] + yd[2])
                    elif c == 1:
                        new = new + couple * xd[0]
                    elif c == 2:
                        new = new + couple * yd[0]
                    else:
                        new = new + row(HEAT) * at(1)
                    new_buf[c, case, x + 2, zs:zs + 8, :] = new
                    if sec == 0:
                        packs[c] = packed(packs[c], new, q)
            for c, value in packs.items():
                ysend[1, c, case] = value
            return 0

        first, last = {None: (0, NX), 0: (0, 4), 1: (2, NX - 2)}[part_of]
        lax.fori_loop(first, last, body, 0, unroll=2)

    def rims(sec, case, comps):
        near, far, cross = {}, {}, {}
        for c in sorted(set(comps) | ({2} if 0 in comps else set()) | ({0} if 2 in comps else set())):
            d = jnp.where(lo_half, yleft[sec, c, case], yright[sec, c, case]) - ysend[sec, c, case]
            p1, m1 = pltpu.roll(d, NY - 1, 1), pltpu.roll(d, 1, 1)
            far_d = jnp.where(lo_half, pltpu.roll(d, NY - 2, 1), pltpu.roll(d, 2, 1))
            near[c] = 16.0 * jnp.where(near1, p1, jnp.where(near2, m1, 0.0)) - far_d
            cross[c] = 8.0 * jnp.where(near1, p1, jnp.where(near2, -m1, 0.0)) + jnp.where(lo_half, -far_d, far_d)
        result = {}
        for c in comps:
            value = pcoef[case, (0, 1, 1, 2)[c]] * near[c]
            if c in (0, 2):
                value = value + pcoef[case, 3] * cross[2 - c]
            result[c] = value
        return result

    def add_rims(sec, case, added, x):
        new_buf = (s1, s0)[sec]
        for c, value in added.items():
            for zt in range(ZT):
                zs = Z0 + 8 * zt
                here = jnp.where(rim, pltpu.roll(value, NY - 2 - 4 * (x * ZT + zt), 1), 0.0)
                new_buf[c, case, x + 2, zs:zs + 8, :] = new_buf[c, case, x + 2, zs:zs + 8, :] + here

    def edges(sec, grps, case, comps):
        new_buf = (s1, s0)[sec]
        added = rims(sec, case, comps)
        for x in (0, 1, NX - 2, NX - 1):
            add_rims(sec, case, added, x)
        if sec == 0:
            for c in comps:
                ysend[1, c, case] = ysend[1, c, case] + added[c]
        for way, ok in ((0, has_down), (1, has_up)):
            @pl.when(ok)
            def _(way=way):
                for grp in grps:
                    x_copy(sec, grp, case, way).wait_recv()
                packs = {c: zero8 for c in comps}
                outer, beside = ((0, 1), (NX - 1, NX - 2))[way]
                slopes = {x: row_of(case, SLOPE, x) for x in (outer, beside)}
                couples = {x: row_of(case, COUPLE, x) for x in (outer, beside)}
                for zt in range(ZT):
                    zs = Z0 + 8 * zt
                    h1, h2 = {}, {}
                    for c in sorted(set(comps) | ({1} if 0 in comps else set()) | ({0} if 1 in comps else set())):
                        first, second = ((1, 0), (0, 1))[way]
                        h1[c] = halo[sec, way, case, c, first, 8 * zt:8 * zt + 8, :]
                        h2[c] = halo[sec, way, case, c, second, 8 * zt:8 * zt + 8, :]
                    for x in (outer, beside):
                        carry = slopes[x] * heights[zt]
                        for c in comps:
                            mate = {0: 1, 1: 0}.get(c)
                            if x == outer:
                                lap = 16.0 * h1[c] - h2[c]
                                grad = lambda k: (h2[k] - 8.0 * h1[k]) if way == 0 else (8.0 * h1[k] - h2[k])
                            else:
                                lap = -h1[c]
                                grad = lambda k: h1[k] if way == 0 else -h1[k]
                            delta = row_of(case, AROW[c], x) * lap + carry * grad(c)
                            if mate is not None:
                                delta = delta + couples[x] * grad(mate)
                            new_buf[c, case, x + 2, zs:zs + 8, :] = new_buf[c, case, x + 2, zs:zs + 8, :] + delta
                            if sec == 0:
                                packs[c] = packed(packs[c], delta, x * ZT + zt)
                if sec == 0:
                    for c in comps:
                        ysend[1, c, case] = ysend[1, c, case] + packs[c]

    def middle(sec, case, comps):
        added = rims(sec, case, comps)

        def body(x, _):
            add_rims(sec, case, added, x)
            return 0

        lax.fori_loop(2, NX - 2, body, 0)

    pltpu.make_async_copy(adjoint, adjoint, in_sem.at[0]).wait()
    for case in range(CASES):
        def pack_rows(x, accs, case=case):
            accs = list(accs)
            for c in range(NC):
                for zt in range(ZT):
                    accs[c] = packed(accs[c], s0[c, case, x + 2, Z0 + 8 * zt:Z0 + 8 * zt + 8, :], x * ZT + zt)
            return tuple(accs)

        accs = lax.fori_loop(0, NX, pack_rows, (zero8,) * NC)
        for c in range(NC):
            ysend[0, c, case] = accs[c]
    pl.semaphore_wait(barrier, plane_n - 1 + ZRING - 1 + 6)
    for case in range(CASES):
        x_start(0, 0, case)
        y_start(0, 0, case)
    pltpu.make_async_copy(source, source, in_sem.at[1]).wait()
    for case in range(CASES):
        inner(0, case, (0, 1, 2))
    for case in range(CASES):
        inner(0, case, (3,))
    for case in range(CASES):
        y_wait(0, 0, case)
        edges(0, (0,), case, (0, 1, 2))
        y_start(1, 0, case)
        x_start(1, 0, case)
    for case in range(CASES):
        y_start(0, 1, case)
        x_start(0, 1, case)
        x_start(1, 1, case)

    def z_sum(buf, c, case, x, weights=None):
        total = None
        for zt in range(ZT):
            tile = buf[c, case, x + 2, Z0 + 8 * zt:Z0 + 8 * zt + 8, :]
            tile = tile if weights is None else tile * weights[zt]
            total = tile if total is None else total + tile
        return jnp.sum(total, axis=0, keepdims=True)

    for side in range(2):
        for case in range(CASES):
            for i in range(2):
                x = (i, NX - 1 - i)[side]
                at = slice(2 * case + i, 2 * case + i + 1)
                zsum[side, 0, at, :] = z_sum(s1, 0, case, x)
                zsum[side, 1, at, :] = z_sum(s1, 2, case, x)
                zsum[side, 2, at, :] = z_sum(s1, 1, case, x)
                zsum[side, 3, at, :] = z_sum(s1, 0, case, x, heights)

    has_row, has_column = (has_down, has_up), (has_right, has_left)

    def corner_copy(side, column):
        return pltpu.make_async_remote_copy(
            src_ref=zsum.at[side, pl.ds(0, 2)], dst_ref=zdiag.at[1 - side, column],
            send_sem=dsend_sem.at[side, column], recv_sem=drecv_sem.at[1 - side, column],
            device_id=corners[side][column], device_id_type=MESH)

    def corner_arrives(side, column):
        return pltpu.make_async_remote_copy(
            src_ref=zsum.at[side, pl.ds(0, 2)], dst_ref=zdiag.at[side, column],
            send_sem=dsend_sem.at[side, column], recv_sem=drecv_sem.at[side, column],
            device_id=corners[side][column], device_id_type=MESH)

    def part_copy(side, slot):
        return pltpu.make_async_remote_copy(
            src_ref=part.at[side], dst_ref=beside.at[slot],
            send_sem=msend_sem.at[side], recv_sem=mrecv_sem.at[slot],
            device_id=(down, up)[side], device_id_type=MESH)

    for side in range(2):
        for column in range(2):
            @pl.when(jnp.logical_and(has_row[side], has_column[column]))
            def _(side=side, column=column):
                corner_copy(side, column).start()

    for case in range(CASES):
        middle(0, case, (0, 1, 2))
    x_sent(0, 0)
    for case in range(CASES):
        inner(1, case, (0, 1), 0)

    def beyond(ghost):
        p1, m1 = pltpu.roll(ghost, NY - 1, 1), pltpu.roll(ghost, 1, 1)
        p2, m2 = pltpu.roll(ghost, NY - 2, 1), pltpu.roll(ghost, 2, 1)
        at0, at_end = lane == 0, lane == NY - 1
        lo, hi = lane < 2, lane >= NY - 2
        near = jnp.where(at_end, p1, jnp.where(at0, m1, 0.0))
        far = jnp.where(hi, p2, jnp.where(lo, m2, 0.0))
        near_x = jnp.where(at_end, p1, jnp.where(at0, -m1, 0.0))
        far_x = jnp.where(hi, p2, jnp.where(lo, -m2, 0.0))
        return 16.0 * near - far, 8.0 * near_x - far_x

    for side in range(2):
        for case in range(CASES):
            for i in range(2):
                x = (i, NX - 1 - i)[side]
                part[side, 0, 2 * case + i:2 * case + i + 1, :] = z_sum(s0, 0, case, x)
        ring_y, _unused = beyond(zsum[side, 0])
        _unused, ring_x = beyond(zsum[side, 1])
        part[side, 0] = part[side, 0] - part[side, 1] * ring_y - part[side, 3] * ring_x

        @pl.when(has_row[side])
        def _(side=side):
            part_copy(side, 1 - side).start()
    for case in range(CASES):
        inner(1, case, (0, 1), 1)

    for case in range(CASES):
        y_wait(1, 0, case)
        edges(1, (0,), case, (0, 1))
        middle(1, case, (0, 1))

        def rows_of(x, _, case=case):
            mean[x + 2, case:case + 1, :] = z_sum(s0, 0, case, x)
            bend = None
            for zt in range(ZT):
                zs = Z0 + 8 * zt
                f = s0[1, case, x + 2, zs:zs + 8, :]
                term = f * (s0[1, case, x + 2, zs + 1:zs + 9, :] - 2.0 * f + s0[1, case, x + 2, zs - 1:zs + 7, :])
                bend = term if bend is None else bend + term
            curv[case, pl.ds(x, 1), :] = jnp.sum(bend, axis=0, keepdims=True)
            return 0

        lax.fori_loop(0, NX, rows_of, 0, unroll=2)

    is_outer = sub % 2 == 0
    for slot in range(2):
        for column in range(2):
            @pl.when(jnp.logical_and(has_row[slot], (has_left, has_right)[column]))
            def _(slot=slot, column=column):
                corner_arrives(slot, column).wait_recv()

        @pl.when(has_row[slot])
        def _(slot=slot):
            part_copy(slot, slot).wait_recv()

            def lap(v, a):
                after, before = pltpu.roll(v, 7, 0), pltpu.roll(v, 1, 0)
                return jnp.where(is_outer, a * v - after, -before)

            sign = (1.0, -1.0)[slot]
            a0, slope, couple = beside[slot, 1], beside[slot, 2], beside[slot, 3]

            def ghost(k):
                return jnp.where(lane >= NY - 2, zdiag[slot, 0, k], jnp.where(lane < 2, zdiag[slot, 1, k], 0.0))

            lap_y, _unused = beyond(ghost(0))
            _unused, grad_y = beyond(ghost(1))
            value = beside[slot, 0] + a0 * (lap(zsum[slot, 0], 16.0) + lap_y)
            value = value + sign * (slope * lap(zsum[slot, 3], 8.0) + couple * lap(zsum[slot, 2], 8.0))
            value = value + couple * grad_y
            for case in range(CASES):
                for i in range(2):
                    row = (1 - i, NX + 2 + i)[slot]
                    mean[row, case:case + 1, :] = value[2 * case + i:2 * case + i + 1, :]

    def store_out(c):
        return [
            pltpu.make_async_copy(
                s0.at[c, :, 2 + x, pl.ds(Z0, NZ), :], out.at[c, :, :, x, :], out_sem.at[c])
            for x in range(NX)
        ]

    grad = jnp.zeros((NX, NY), jnp.float32)
    for case in range(CASES):
        theta = THETA_STEP * temp[case].astype(jnp.float32)
        visc = jnp.exp(VISCOSITY_PRESS * pressure[case] - VISCOSITY_TEMP * theta)
        density = 1.0 - 0.6 * cavity[case].astype(jnp.float32)

        def rows(dx):
            return mean[2 + dx:2 + dx + NX, case, :]

        slope = (8.0 * (rows(1) - rows(-1)) - (rows(2) - rows(-2))) / (12.0 * NZ)
        grad = grad + (density * thick / 2.0 * slope
                       - 8.0 * visc / (thick * thick * thick) * (curv[case] / NZ))
    wall[...] = grad
    mine[0] = jnp.sum(grad * grad, axis=0, keepdims=True)

    def plane_copy(o):
        return pltpu.make_async_remote_copy(
            src_ref=mine.at[0], dst_ref=plane.at[o], send_sem=rsend_sem.at[0], recv_sem=rrecv_sem.at[0],
            device_id=plane_peer(o), device_id_type=MESH)

    def ring_copy(o):
        return pltpu.make_async_remote_copy(
            src_ref=mine2.at[0], dst_ref=ring.at[o], send_sem=rsend_sem.at[1], recv_sem=rrecv_sem.at[1],
            device_id=ring_peer(o), device_id_type=MESH)

    def hops(o):
        dt = o // (2 * groups)
        return min(dt % 4, 4 - dt % 4) + 2 * (dt >= 4) + (o // 2) % groups

    for o in sorted(range(1, plane_n), key=lambda o: -hops(o)):
        plane_copy(o).start()

    for case in range(CASES):
        y_wait(0, 1, case)
        edges(0, (1,), case, (3,))
        y_start(1, 1, case)
        x_start(1, 2, case)
    for c in (0, 1):
        for copy in store_out(c):
            copy.start()
    for case in range(CASES):
        middle(0, case, (3,))
    x_sent(0, 1)
    for case in range(CASES):
        inner(1, case, (2, 3))
    pltpu.make_async_copy(plane.at[pl.ds(1, plane_n - 1)], plane.at[pl.ds(1, plane_n - 1)], rrecv_sem.at[0]).wait()
    mine2[0] = mine[0] + jnp.sum(plane[1:plane_n], axis=0)
    for o in sorted(range(1, ZRING), key=lambda o: -min(o, ZRING - o)):
        ring_copy(o).start()
    for case in range(CASES):
        y_wait(1, 1, case)
        edges(1, (1, 2), case, (2, 3))
        middle(1, case, (2, 3))
    for c in (2, 3):
        for copy in store_out(c):
            copy.start()
    pltpu.make_async_copy(ring.at[pl.ds(1, ZRING - 1)], ring.at[pl.ds(1, ZRING - 1)], rrecv_sem.at[1]).wait()
    total = jnp.sum(mine2[0] + jnp.sum(ring[1:ZRING], axis=0), axis=1, keepdims=True)
    wall[...] = wall[...] / jnp.sqrt(total / cells + 1e-06)

    pltpu.make_async_copy(plane.at[pl.ds(1, plane_n - 1)], plane.at[pl.ds(1, plane_n - 1)], rsend_sem.at[0]).wait()
    pltpu.make_async_copy(ring.at[pl.ds(1, ZRING - 1)], ring.at[pl.ds(1, ZRING - 1)], rsend_sem.at[1]).wait()
    for side in range(2):
        @pl.when(has_row[side])
        def _(side=side):
            part_copy(side, 1 - side).wait_send()
        for column in range(2):
            @pl.when(jnp.logical_and(has_row[side], has_column[column]))
            def _(side=side, column=column):
                corner_copy(side, column).wait_send()
    for grp in range(3):
        x_sent(1, grp)
    for sec in range(2):
        y_sent(sec)
    for c in range(NC):
        pltpu.make_async_copy(out.at[c], out.at[c], out_sem.at[c]).wait()


def on_device(adjoint, source, pressure, film, cavity, temp_index):
    vmem = pl.BlockSpec(memory_space=pltpu.VMEM)
    hbm = pl.BlockSpec(memory_space=pltpu.HBM)
    f32 = jnp.float32
    dma = pltpu.SemaphoreType.DMA
    given = [
        pltpu.with_memory_space_constraint(a, pltpu.HBM)
        for a in (adjoint, source, pressure, film, cavity, temp_index)
    ]
    return pl.pallas_call(
        kernel,
        out_shape=(pltpu.VMEM(adjoint.shape, f32), pltpu.VMEM(film.shape, f32)),
        in_specs=[hbm] * 6,
        out_specs=(vmem, vmem),
        scratch_shapes=[
            pltpu.VMEM(pressure.shape, f32),
            pltpu.VMEM(film.shape, f32),
            pltpu.VMEM(cavity.shape, jnp.int32),
            pltpu.SMEM(temp_index.shape, jnp.int32),
            pltpu.VMEM((NC, CASES, NX + 4, ZROWS, NY), f32),
            pltpu.VMEM((NC, CASES, NX + 4, ZROWS, NY), f32),
            pltpu.VMEM((2, 2, CASES, NC, 2, NZ, NY), f32),
            pltpu.VMEM((NC, CASES, NX, NZ, NY), f32),
            pltpu.VMEM((CASES, 13, NX, NY), f32),
            pltpu.VMEM((CASES, 4, 8, NY), f32),
            pltpu.VMEM((2, NC, CASES, 8, NY), f32),
            pltpu.VMEM((2, NC, CASES, 8, NY), f32),
            pltpu.VMEM((2, NC, CASES, 8, NY), f32),
            pltpu.VMEM((NX + 4, CASES, NY), f32),
            pltpu.VMEM((CASES, NX, NY), f32),
            pltpu.VMEM((2, 4, 8, NY), f32),
            pltpu.VMEM((2, 2, 2, 8, NY), f32),
            pltpu.VMEM((2, 4, 8, NY), f32),
            pltpu.VMEM((2, 4, 8, NY), f32),
            pltpu.VMEM((1, 1, NY), f32),
            pltpu.VMEM((32, 1, NY), f32),
            pltpu.VMEM((1, 1, NY), f32),
            pltpu.VMEM((ZRING, 1, NY), f32),
            dma((4,)),
            dma((2,)),
            dma((NC,)),
            dma((2, 3, 2)),
            dma((2, 3, CASES, 2)),
            dma((2, 2)),
            dma((2, 2, CASES, 2)),
            dma((2,)),
            dma((2,)),
            dma((2, 2)),
            dma((2, 2)),
            dma((2,)),
            dma((2,)),
        ],
        compiler_params=pltpu.CompilerParams(
            collective_id=0, has_side_effects=True, vmem_limit_bytes=48 * 1024 * 1024
        ),
        name="lubrication_adjoint",
    )(*given)


def solution(mesh):
    placed = (
        P(None, None, None, "roll", "trans"),
        P(None, None, None, "roll", "trans"),
        P(None, "roll", "trans"),
        P("roll", "trans"),
        P(None, "roll", "trans"),
        P(),
    )
    return jax.shard_map(
        on_device,
        mesh=mesh,
        in_specs=placed,
        out_specs=(P(None, None, None, "roll", "trans"), P("roll", "trans")),
        check_vma=False,
    )
```

```python
import jax
import jax.numpy as jnp
from jax import lax
from jax.experimental import pallas as pl
from jax.experimental.pallas import tpu as pltpu
from jax.sharding import PartitionSpec as P

VISCOSITY_PRESS = 0.3
VISCOSITY_TEMP = 0.5
THETA_STEP = 0.2
SOUND = 0.5
KAPPA = 0.6
HEATING = 0.3
COURANT = 0.8

MESH = pl.DeviceIdType.MESH
NC = 4
CASES = 2
NZ = 32
NX = 8
NY = 128
Z0 = 8
ZROWS = 48
ZT = NZ // 8
ZRING = 8
XGROUPS = (((0, 3), (3, 1)), ((0, 2), (2, 1), (3, 1)))
YGROUPS = (((0, 3), (3, 1)), ((0, 3), (3, 1)))

STEP, SLOPE, COUPLE, HEAT, A0, A1, A3, B0, B1, B3, C0, C1, C3 = range(13)
AROW = (A0, A1, A1, A3)
BROW = (B0, B1, B1, B3)
CROW = (C0, C1, C1, C3)


def kernel(
    adjoint, source, pressure_in, film_in, cavity_in, temp_in, out, wall,
    pressure, film, cavity, temp,
    s0, s1, halo, src, coef, pcoef, ysend, yleft, yright, mean, curv, zsum, zdiag, part, beside, mine, plane, mine2, ring,
    small_sem, in_sem, out_sem, xsend_sem, xrecv_sem, ysend_sem, yrecv_sem,
    msend_sem, mrecv_sem, dsend_sem, drecv_sem, rsend_sem, rrecv_sem, word,
):
    nr, nt = lax.axis_size("roll"), lax.axis_size("trans")
    r, t = lax.axis_index("roll"), lax.axis_index("trans")
    core = lax.rem(r, 2)
    z = lax.rem(r // 2, ZRING)
    g = r // (2 * ZRING)
    groups = nr // (2 * ZRING)
    plane_n = groups * 2 * nt
    cells = nr * NX * nt * NY

    def plane_peer(o):
        dt, dg, dc = o // (2 * groups), (o // 2) % groups, o % 2
        row = (lax.rem(g + dg, groups) * ZRING + z) * 2 + lax.rem(core + dc, 2)
        return (row, lax.rem(t + dt, nt))

    def ring_peer(o):
        return ((g * ZRING + lax.rem(z + o, ZRING)) * 2 + core, t)

    up = (lax.rem(r + 1, nr), t)
    down = (lax.rem(r + nr - 1, nr), t)
    right = (r, lax.rem(t + 1, nt))
    left = (r, lax.rem(t + nt - 1, nt))
    has_up, has_down = r < nr - 1, r > 0
    has_right, has_left = t < nt - 1, t > 0

    barrier = pltpu.get_barrier_semaphore()
    def hops(o):
        dt = o // (2 * groups)
        return min(dt % 4, 4 - dt % 4) + 2 * (dt >= 4) + (o // 2) % groups

    far_plane = sorted(range(1, plane_n), key=lambda o: -hops(o))
    far_ring = sorted(range(1, ZRING), key=lambda o: -min(o, ZRING - o))
    corners = [[(row[0], column[1]) for column in (right, left)] for row in (down, up)]
    y_phys = 2 * (t // 4) + g

    def in_plane(dx, dy, dc):
        y = lax.rem(y_phys + dy + 4, 4)
        row = ((lax.rem(y, 2)) * ZRING + z) * 2 + lax.rem(core + dc, 2)
        return (row, (y // 2) * 4 + lax.rem(lax.rem(t, 4) + dx + 4, 4))

    close = [
        in_plane(dx, dy, dc)
        for dx in (2, 1, -1, 0) for dy in (2, 1, -1, 0) for dc in (1, 0)
        if (dx, dy, dc) != (0, 0, 0) and abs(dx) + abs(dy) <= 2
    ]
    partners = [right, left, up, down] + [ring_peer(o) for o in (2, ZRING - 2, 1, ZRING - 1)] + close
    for peer in partners:
        pl.semaphore_signal(barrier, inc=1, device_id=peer, device_id_type=MESH)

    smalls = [
        pltpu.make_async_copy(given, held, small_sem.at[k])
        for k, (given, held) in enumerate(
            ((pressure_in, pressure), (film_in, film), (cavity_in, cavity), (temp_in, temp)))
    ]
    loads = [
        pltpu.make_async_copy(
            adjoint.at[:, :, :, x, :], s0.at[:, :, 2 + x, pl.ds(Z0, NZ), :], in_sem.at[0])
        for x in range(NX)
    ]
    src_loads = [
        pltpu.make_async_copy(source.at[:, :, :, x, :], src.at[:, :, x], in_sem.at[1])
        for x in range(NX)
    ]
    for copy in smalls + loads + src_loads:
        copy.start()

    lane = lax.broadcasted_iota(jnp.int32, (8, NY), 1)
    sub = lax.broadcasted_iota(jnp.int32, (8, NY), 0)
    lane4, lane_in4 = lane // 4, lane % 4
    lo_half = lane_in4 < 2
    near1, near2 = lane_in4 == 1, lane_in4 == 2
    rim = jnp.logical_or(lane < 2, lane >= NY - 2)
    heights = [(sub.astype(jnp.float32) + (8 * zt + 0.5)) / NZ for zt in range(ZT)]
    zero8 = jnp.zeros((8, NY), jnp.float32)

    for buf in (s0, s1):
        def clear(i, _, buf=buf):
            for case in range(CASES):
                for c in range(NC):
                    buf[c, case, i, 0:Z0, :] = zero8
                    buf[c, case, i, Z0 + NZ:ZROWS, :] = zero8
            return 0
        lax.fori_loop(0, NX + 4, clear, 0)

        def clear_row(i, _, buf=buf):
            for case in range(CASES):
                for x in (0, 1, NX + 2, NX + 3):
                    for zt in range(ZT):
                        buf[i, case, x, Z0 + 8 * zt:Z0 + 8 * zt + 8, :] = zero8
            return 0
        lax.fori_loop(0, NC, clear_row, 0)

    def clear_pack(i, _):
        for case in range(CASES):
            ysend[1, i, case] = zero8
        return 0
    lax.fori_loop(0, NC, clear_pack, 0)

    @pl.when(jnp.logical_not(has_down))
    def _():
        mean[0:2] = jnp.zeros((2, CASES, NY), jnp.float32)

    @pl.when(jnp.logical_not(has_up))
    def _():
        mean[NX + 2:NX + 4] = jnp.zeros((2, CASES, NY), jnp.float32)

    @pl.when(jnp.logical_not(has_left))
    def _():
        yleft[...] = jnp.zeros(yleft.shape, jnp.float32)
        zdiag[:, 0] = jnp.zeros((2, 2, 8, NY), jnp.float32)

    @pl.when(jnp.logical_not(has_right))
    def _():
        yright[...] = jnp.zeros(yright.shape, jnp.float32)
        zdiag[:, 1] = jnp.zeros((2, 2, 8, NY), jnp.float32)

    for copy in smalls:
        copy.wait()
    thick = film[...]
    for case in range(CASES):
        theta = THETA_STEP * temp[case].astype(jnp.float32)
        visc = jnp.exp(VISCOSITY_PRESS * pressure[case] - VISCOSITY_TEMP * theta)
        fcoef = 4.0 * visc / (thick * thick)
        density = 1.0 - 0.6 * cavity[case].astype(jnp.float32)
        step = COURANT / (32.0 / 3.0 * visc + 4.0 * fcoef + 2.0 * SOUND + 1.0)
        sv, sf = step * visc, step * fcoef
        table = {
            STEP: step, SLOPE: step * density / 12.0, COUPLE: step * (SOUND / 12.0), HEAT: HEATING * sv,
        }
        for scale, a, b, c in ((0.5, A0, B0, C0), (1.0, A1, B1, C1), (KAPPA, A3, B3, C3)):
            table[a] = (scale / 12.0) * sv
            table[b] = scale * sf
            table[c] = 1.0 - scale * (5.0 * sv + 2.0 * sf)
        for k, value in table.items():
            coef[case, k] = value
        for k, value in ((0, sv), (1, step)):
            acc = zero8
            for x in range(NX):
                here = jnp.logical_and(lane4 == ZT * x, sub == x)
                acc = jnp.where(here, pltpu.roll(value, 4 * ZT * x + 2, 1), acc)
            acc = acc + pltpu.roll(acc, 4, 1)
            acc = acc + pltpu.roll(acc, 8, 1)
            spread = jnp.broadcast_to(jnp.sum(acc, axis=0, keepdims=True), (8, NY))
            if k == 0:
                pcoef[case, 0] = (0.5 / 12.0) * spread
                pcoef[case, 1] = (1.0 / 12.0) * spread
                pcoef[case, 2] = (KAPPA / 12.0) * spread
            else:
                pcoef[case, 3] = (SOUND / 12.0) * spread

    for side in range(2):
        for k in range(4):
            zsum[side, k] = zero8
            part[side, k] = zero8
        for case in range(CASES):
            for i in range(2):
                x = (i, NX - 1 - i)[side]
                for j, k in enumerate((A0, SLOPE, COUPLE)):
                    part[side, 1 + j, 2 * case + i:2 * case + i + 1, :] = coef[case, k, x:x + 1, :]

    def x_copy(sec, grp, case, way):
        buf = (s0, s1)[sec]
        c, n = XGROUPS[sec][grp]
        a, peer = ((NX, up), (2, down))[way]
        return pltpu.make_async_remote_copy(
            src_ref=buf.at[pl.ds(c, n), case, pl.ds(a, 2), pl.ds(Z0, NZ), :],
            dst_ref=halo.at[sec, way, case, pl.ds(c, n)],
            send_sem=xsend_sem.at[sec, grp, way],
            recv_sem=xrecv_sem.at[sec, grp, case, way],
            device_id=peer, device_id_type=MESH)

    def y_copy(sec, grp, case, way):
        c, n = YGROUPS[sec][grp]
        dst, peer = ((yleft, right), (yright, left))[way]
        return pltpu.make_async_remote_copy(
            src_ref=ysend.at[sec, pl.ds(c, n), case],
            dst_ref=dst.at[sec, pl.ds(c, n), case],
            send_sem=ysend_sem.at[sec, way],
            recv_sem=yrecv_sem.at[sec, grp, case, way],
            device_id=peer, device_id_type=MESH)

    def x_start(sec, grp, case):
        for way, ok in ((0, has_up), (1, has_down)):
            @pl.when(ok)
            def _(way=way):
                x_copy(sec, grp, case, way).start()

    def y_start(sec, grp, case):
        for way, ok in ((0, has_right), (1, has_left)):
            @pl.when(ok)
            def _(way=way):
                y_copy(sec, grp, case, way).start()

    def y_wait(sec, grp, case):
        for way, ok in ((0, has_left), (1, has_right)):
            @pl.when(ok)
            def _(way=way):
                y_copy(sec, grp, case, way).wait_recv()

    def x_sent(sec, grp):
        c, n = XGROUPS[sec][grp]
        for way, ok in ((0, has_up), (1, has_down)):
            @pl.when(ok)
            def _(way=way):
                both = halo.at[sec, way, :, pl.ds(c, n)]
                pltpu.make_async_copy(both, both, xsend_sem.at[sec, grp, way]).wait()

    def y_sent(sec):
        for way, ok in ((0, has_right), (1, has_left)):
            @pl.when(ok)
            def _(way=way):
                pltpu.make_async_copy(ysend.at[sec], ysend.at[sec], ysend_sem.at[sec, way]).wait()

    def row_of(case, k, x):
        return jnp.broadcast_to(coef[case, k, pl.ds(x, 1), :], (8, NY))

    def packed(acc, tile, q):
        return jnp.where(lane4 == q, pltpu.roll(tile, 4 * q + 2, 1), acc)

    def inner(sec, case, comps, part_of=None):
        cur, new_buf = ((s0, s1), (s1, s0))[sec]
        need_x = sorted(set(comps) | ({1} if 0 in comps else set()) | ({0} if 1 in comps else set()))
        need_y = sorted(set(comps) | ({2} if 0 in comps else set()) | ({0} if 2 in comps else set()))

        def body(i, _):
            x = i + 4 * (i // 2) if part_of == 0 else i

            def row(k):
                return row_of(case, k, x)

            step, slope, couple = row(STEP), row(SLOPE), row(COUPLE)
            packs = {}
            if sec == 0:
                packs = {c: ysend[1, c, case] for c in comps}
            for zt in range(ZT):
                zs = Z0 + 8 * zt
                q = x * ZT + zt
                carry = slope * heights[zt]

                def at(c, dx=0, dz=0):
                    return cur[c, case, x + 2 + dx, zs + dz:zs + dz + 8, :]

                xd, yd, e1, e2 = {}, {}, {}, {}
                for c in need_y:
                    f = at(c)
                    p1, m1 = pltpu.roll(f, NY - 1, 1), pltpu.roll(f, 1, 1)
                    p2, m2 = pltpu.roll(f, NY - 2, 1), pltpu.roll(f, 2, 1)
                    if (c == 2 and 0 in comps) or (c == 0 and 2 in comps):
                        yd[c] = 8.0 * (p1 - m1) - (p2 - m2)
                    e1[c], e2[c] = p1 + m1, p2 + m2
                for c in need_x:
                    p1, m1, p2, m2 = at(c, 1), at(c, -1), at(c, 2), at(c, -2)
                    xd[c] = 8.0 * (p1 - m1) - (p2 - m2)
                    if c in comps:
                        e1[c], e2[c] = e1[c] + (p1 + m1), e2[c] + (p2 + m2)
                for c in comps:
                    new = row(CROW[c]) * at(c) + row(AROW[c]) * (16.0 * e1[c] - e2[c])
                    new = new + row(BROW[c]) * (at(c, 0, 1) + at(c, 0, -1))
                    new = new + (carry * xd[c] + step * src[c, case, x, 8 * zt:8 * zt + 8, :])
                    if c == 0:
                        new = new + couple * (xd[1] + yd[2])
                    elif c == 1:
                        new = new + couple * xd[0]
                    elif c == 2:
                        new = new + couple * yd[0]
                    else:
                        new = new + row(HEAT) * at(1)
                    new_buf[c, case, x + 2, zs:zs + 8, :] = new
                    if sec == 0:
                        packs[c] = packed(packs[c], new, q)
            for c, value in packs.items():
                ysend[1, c, case] = value
            return 0

        first, last = {None: (0, NX), 0: (0, 4), 1: (2, NX - 2)}[part_of]
        lax.fori_loop(first, last, body, 0, unroll=2)

    def rims(sec, case, comps):
        near, far, cross = {}, {}, {}
        for c in sorted(set(comps) | ({2} if 0 in comps else set()) | ({0} if 2 in comps else set())):
            d = jnp.where(lo_half, yleft[sec, c, case], yright[sec, c, case]) - ysend[sec, c, case]
            p1, m1 = pltpu.roll(d, NY - 1, 1), pltpu.roll(d, 1, 1)
            far_d = jnp.where(lo_half, pltpu.roll(d, NY - 2, 1), pltpu.roll(d, 2, 1))
            near[c] = 16.0 * jnp.where(near1, p1, jnp.where(near2, m1, 0.0)) - far_d
            cross[c] = 8.0 * jnp.where(near1, p1, jnp.where(near2, -m1, 0.0)) + jnp.where(lo_half, -far_d, far_d)
        result = {}
        for c in comps:
            value = pcoef[case, (0, 1, 1, 2)[c]] * near[c]
            if c in (0, 2):
                value = value + pcoef[case, 3] * cross[2 - c]
            result[c] = value
        return result

    def add_rims(sec, case, added, x):
        new_buf = (s1, s0)[sec]
        for c, value in added.items():
            for zt in range(ZT):
                zs = Z0 + 8 * zt
                here = jnp.where(rim, pltpu.roll(value, NY - 2 - 4 * (x * ZT + zt), 1), 0.0)
                new_buf[c, case, x + 2, zs:zs + 8, :] = new_buf[c, case, x + 2, zs:zs + 8, :] + here

    def edges(sec, grps, case, comps):
        new_buf = (s1, s0)[sec]
        added = rims(sec, case, comps)
        for x in (0, 1, NX - 2, NX - 1):
            add_rims(sec, case, added, x)
        if sec == 0:
            for c in comps:
                ysend[1, c, case] = ysend[1, c, case] + added[c]
        for way, ok in ((0, has_down), (1, has_up)):
            @pl.when(ok)
            def _(way=way):
                for grp in grps:
                    x_copy(sec, grp, case, way).wait_recv()
                packs = {c: zero8 for c in comps}
                outer, beside = ((0, 1), (NX - 1, NX - 2))[way]
                slopes = {x: row_of(case, SLOPE, x) for x in (outer, beside)}
                couples = {x: row_of(case, COUPLE, x) for x in (outer, beside)}
                for zt in range(ZT):
                    zs = Z0 + 8 * zt
                    h1, h2 = {}, {}
                    for c in sorted(set(comps) | ({1} if 0 in comps else set()) | ({0} if 1 in comps else set())):
                        first, second = ((1, 0), (0, 1))[way]
                        h1[c] = halo[sec, way, case, c, first, 8 * zt:8 * zt + 8, :]
                        h2[c] = halo[sec, way, case, c, second, 8 * zt:8 * zt + 8, :]
                    for x in (outer, beside):
                        carry = slopes[x] * heights[zt]
                        for c in comps:
                            mate = {0: 1, 1: 0}.get(c)
                            if x == outer:
                                lap = 16.0 * h1[c] - h2[c]
                                grad = lambda k: (h2[k] - 8.0 * h1[k]) if way == 0 else (8.0 * h1[k] - h2[k])
                            else:
                                lap = -h1[c]
                                grad = lambda k: h1[k] if way == 0 else -h1[k]
                            delta = row_of(case, AROW[c], x) * lap + carry * grad(c)
                            if mate is not None:
                                delta = delta + couples[x] * grad(mate)
                            new_buf[c, case, x + 2, zs:zs + 8, :] = new_buf[c, case, x + 2, zs:zs + 8, :] + delta
                            if sec == 0:
                                packs[c] = packed(packs[c], delta, x * ZT + zt)
                if sec == 0:
                    for c in comps:
                        ysend[1, c, case] = ysend[1, c, case] + packs[c]

    def middle(sec, case, comps):
        added = rims(sec, case, comps)

        def body(x, _):
            add_rims(sec, case, added, x)
            return 0

        lax.fori_loop(2, NX - 2, body, 0)

    pltpu.make_async_copy(adjoint, adjoint, in_sem.at[0]).wait()
    for case in range(CASES):
        def pack_rows(x, accs, case=case):
            accs = list(accs)
            for c in range(NC):
                for zt in range(ZT):
                    accs[c] = packed(accs[c], s0[c, case, x + 2, Z0 + 8 * zt:Z0 + 8 * zt + 8, :], x * ZT + zt)
            return tuple(accs)

        accs = lax.fori_loop(0, NX, pack_rows, (zero8,) * NC)
        for c in range(NC):
            ysend[0, c, case] = accs[c]
    pl.semaphore_wait(barrier, len(partners))
    for case in range(CASES):
        y_start(0, 0, case)
    for case in range(CASES):
        x_start(0, 0, case)
    for peer in partners:
        pl.semaphore_signal(word, inc=1, device_id=peer, device_id_type=MESH)
    pltpu.make_async_copy(source, source, in_sem.at[1]).wait()
    for case in range(CASES):
        inner(0, case, (0, 1, 2))
    for case in range(CASES):
        inner(0, case, (3,))
    for case in range(CASES):
        y_wait(0, 0, case)
        edges(0, (0,), case, (0, 1, 2))
        y_start(1, 0, case)
        x_start(1, 0, case)
    for case in range(CASES):
        y_start(0, 1, case)
        x_start(0, 1, case)
        x_start(1, 1, case)

    pl.semaphore_wait(word, len(partners))

    def z_sum(buf, c, case, x, weights=None):
        total = None
        for zt in range(ZT):
            tile = buf[c, case, x + 2, Z0 + 8 * zt:Z0 + 8 * zt + 8, :]
            tile = tile if weights is None else tile * weights[zt]
            total = tile if total is None else total + tile
        return jnp.sum(total, axis=0, keepdims=True)

    for side in range(2):
        for case in range(CASES):
            for i in range(2):
                x = (i, NX - 1 - i)[side]
                at = slice(2 * case + i, 2 * case + i + 1)
                zsum[side, 0, at, :] = z_sum(s1, 0, case, x)
                zsum[side, 1, at, :] = z_sum(s1, 2, case, x)
                zsum[side, 2, at, :] = z_sum(s1, 1, case, x)
                zsum[side, 3, at, :] = z_sum(s1, 0, case, x, heights)

    has_row, has_column = (has_down, has_up), (has_right, has_left)

    def corner_copy(side, column):
        return pltpu.make_async_remote_copy(
            src_ref=zsum.at[side, pl.ds(0, 2)], dst_ref=zdiag.at[1 - side, column],
            send_sem=dsend_sem.at[side, column], recv_sem=drecv_sem.at[1 - side, column],
            device_id=corners[side][column], device_id_type=MESH)

    def corner_arrives(side, column):
        return pltpu.make_async_remote_copy(
            src_ref=zsum.at[side, pl.ds(0, 2)], dst_ref=zdiag.at[side, column],
            send_sem=dsend_sem.at[side, column], recv_sem=drecv_sem.at[side, column],
            device_id=corners[side][column], device_id_type=MESH)

    def part_copy(side, slot):
        return pltpu.make_async_remote_copy(
            src_ref=part.at[side], dst_ref=beside.at[slot],
            send_sem=msend_sem.at[side], recv_sem=mrecv_sem.at[slot],
            device_id=(down, up)[side], device_id_type=MESH)

    for side in range(2):
        for column in range(2):
            @pl.when(jnp.logical_and(has_row[side], has_column[column]))
            def _(side=side, column=column):
                corner_copy(side, column).start()

    for case in range(CASES):
        middle(0, case, (0, 1, 2))
    x_sent(0, 0)
    for case in range(CASES):
        inner(1, case, (0, 1), 0)

    def beyond(ghost):
        p1, m1 = pltpu.roll(ghost, NY - 1, 1), pltpu.roll(ghost, 1, 1)
        p2, m2 = pltpu.roll(ghost, NY - 2, 1), pltpu.roll(ghost, 2, 1)
        at0, at_end = lane == 0, lane == NY - 1
        lo, hi = lane < 2, lane >= NY - 2
        near = jnp.where(at_end, p1, jnp.where(at0, m1, 0.0))
        far = jnp.where(hi, p2, jnp.where(lo, m2, 0.0))
        near_x = jnp.where(at_end, p1, jnp.where(at0, -m1, 0.0))
        far_x = jnp.where(hi, p2, jnp.where(lo, -m2, 0.0))
        return 16.0 * near - far, 8.0 * near_x - far_x

    for side in range(2):
        for case in range(CASES):
            for i in range(2):
                x = (i, NX - 1 - i)[side]
                part[side, 0, 2 * case + i:2 * case + i + 1, :] = z_sum(s0, 0, case, x)
        ring_y, _unused = beyond(zsum[side, 0])
        _unused, ring_x = beyond(zsum[side, 1])
        part[side, 0] = part[side, 0] - part[side, 1] * ring_y - part[side, 3] * ring_x

        @pl.when(has_row[side])
        def _(side=side):
            part_copy(side, 1 - side).start()
    for case in range(CASES):
        inner(1, case, (0, 1), 1)

    for case in range(CASES):
        y_wait(1, 0, case)
        edges(1, (0,), case, (0, 1))
        middle(1, case, (0, 1))

        def rows_of(x, _, case=case):
            mean[x + 2, case:case + 1, :] = z_sum(s0, 0, case, x)
            bend = None
            for zt in range(ZT):
                zs = Z0 + 8 * zt
                f = s0[1, case, x + 2, zs:zs + 8, :]
                term = f * (s0[1, case, x + 2, zs + 1:zs + 9, :] - 2.0 * f + s0[1, case, x + 2, zs - 1:zs + 7, :])
                bend = term if bend is None else bend + term
            curv[case, pl.ds(x, 1), :] = jnp.sum(bend, axis=0, keepdims=True)
            return 0

        lax.fori_loop(0, NX, rows_of, 0, unroll=2)

    is_outer = sub % 2 == 0
    for slot in range(2):
        for column in range(2):
            @pl.when(jnp.logical_and(has_row[slot], (has_left, has_right)[column]))
            def _(slot=slot, column=column):
                corner_arrives(slot, column).wait_recv()

        @pl.when(has_row[slot])
        def _(slot=slot):
            part_copy(slot, slot).wait_recv()

            def lap(v, a):
                after, before = pltpu.roll(v, 7, 0), pltpu.roll(v, 1, 0)
                return jnp.where(is_outer, a * v - after, -before)

            sign = (1.0, -1.0)[slot]
            a0, slope, couple = beside[slot, 1], beside[slot, 2], beside[slot, 3]

            def ghost(k):
                return jnp.where(lane >= NY - 2, zdiag[slot, 0, k], jnp.where(lane < 2, zdiag[slot, 1, k], 0.0))

            lap_y, _unused = beyond(ghost(0))
            _unused, grad_y = beyond(ghost(1))
            value = beside[slot, 0] + a0 * (lap(zsum[slot, 0], 16.0) + lap_y)
            value = value + sign * (slope * lap(zsum[slot, 3], 8.0) + couple * lap(zsum[slot, 2], 8.0))
            value = value + couple * grad_y
            for case in range(CASES):
                for i in range(2):
                    row = (1 - i, NX + 2 + i)[slot]
                    mean[row, case:case + 1, :] = value[2 * case + i:2 * case + i + 1, :]

    def store_out(c):
        return [
            pltpu.make_async_copy(
                s0.at[c, :, 2 + x, pl.ds(Z0, NZ), :], out.at[c, :, :, x, :], out_sem.at[c])
            for x in range(NX)
        ]

    grad = jnp.zeros((NX, NY), jnp.float32)
    for case in range(CASES):
        theta = THETA_STEP * temp[case].astype(jnp.float32)
        visc = jnp.exp(VISCOSITY_PRESS * pressure[case] - VISCOSITY_TEMP * theta)
        density = 1.0 - 0.6 * cavity[case].astype(jnp.float32)

        def rows(dx):
            return mean[2 + dx:2 + dx + NX, case, :]

        slope = (8.0 * (rows(1) - rows(-1)) - (rows(2) - rows(-2))) / (12.0 * NZ)
        grad = grad + (density * thick / 2.0 * slope
                       - 8.0 * visc / (thick * thick * thick) * (curv[case] / NZ))
    wall[...] = grad
    mine[0] = jnp.sum(grad * grad, axis=0, keepdims=True)

    def plane_copy(o):
        return pltpu.make_async_remote_copy(
            src_ref=mine.at[0], dst_ref=plane.at[o], send_sem=rsend_sem.at[0], recv_sem=rrecv_sem.at[0],
            device_id=plane_peer(o), device_id_type=MESH)

    def ring_copy(o):
        return pltpu.make_async_remote_copy(
            src_ref=mine2.at[0], dst_ref=ring.at[o], send_sem=rsend_sem.at[1], recv_sem=rrecv_sem.at[1],
            device_id=ring_peer(o), device_id_type=MESH)

    for o in far_plane:
        plane_copy(o).start()

    for case in range(CASES):
        y_wait(0, 1, case)
        edges(0, (1,), case, (3,))
        y_start(1, 1, case)
        x_start(1, 2, case)
    for c in (0, 1):
        for copy in store_out(c):
            copy.start()
    for case in range(CASES):
        middle(0, case, (3,))
    x_sent(0, 1)
    for case in range(CASES):
        inner(1, case, (2, 3))
    pltpu.make_async_copy(plane.at[pl.ds(1, plane_n - 1)], plane.at[pl.ds(1, plane_n - 1)], rrecv_sem.at[0]).wait()
    mine2[0] = mine[0] + jnp.sum(plane[1:plane_n], axis=0)
    for o in far_ring:
        ring_copy(o).start()
    for case in range(CASES):
        y_wait(1, 1, case)
        edges(1, (1, 2), case, (2, 3))
        middle(1, case, (2, 3))
    for c in (2, 3):
        for copy in store_out(c):
            copy.start()
    pltpu.make_async_copy(plane.at[pl.ds(1, plane_n - 1)], plane.at[pl.ds(1, plane_n - 1)], rsend_sem.at[0]).wait()
    pltpu.make_async_copy(ring.at[pl.ds(1, ZRING - 1)], ring.at[pl.ds(1, ZRING - 1)], rsend_sem.at[1]).wait()
    for side in range(2):
        @pl.when(has_row[side])
        def _(side=side):
            part_copy(side, 1 - side).wait_send()
        for column in range(2):
            @pl.when(jnp.logical_and(has_row[side], has_column[column]))
            def _(side=side, column=column):
                corner_copy(side, column).wait_send()
    for grp in range(3):
        x_sent(1, grp)
    for sec in range(2):
        y_sent(sec)
    for c in range(NC):
        pltpu.make_async_copy(out.at[c], out.at[c], out_sem.at[c]).wait()

    pltpu.make_async_copy(ring.at[pl.ds(1, ZRING - 1)], ring.at[pl.ds(1, ZRING - 1)], rrecv_sem.at[1]).wait()
    total = jnp.sum(mine2[0] + jnp.sum(ring[1:ZRING], axis=0), axis=1, keepdims=True)
    wall[...] = wall[...] / jnp.sqrt(total / cells + 1e-06)


def on_device(adjoint, source, pressure, film, cavity, temp_index):
    vmem = pl.BlockSpec(memory_space=pltpu.VMEM)
    hbm = pl.BlockSpec(memory_space=pltpu.HBM)
    f32 = jnp.float32
    dma = pltpu.SemaphoreType.DMA
    given = [
        pltpu.with_memory_space_constraint(a, pltpu.HBM)
        for a in (adjoint, source, pressure, film, cavity, temp_index)
    ]
    return pl.pallas_call(
        kernel,
        out_shape=(pltpu.VMEM(adjoint.shape, f32), pltpu.VMEM(film.shape, f32)),
        in_specs=[hbm] * 6,
        out_specs=(vmem, vmem),
        scratch_shapes=[
            pltpu.VMEM(pressure.shape, f32),
            pltpu.VMEM(film.shape, f32),
            pltpu.VMEM(cavity.shape, jnp.int32),
            pltpu.SMEM(temp_index.shape, jnp.int32),
            pltpu.VMEM((NC, CASES, NX + 4, ZROWS, NY), f32),
            pltpu.VMEM((NC, CASES, NX + 4, ZROWS, NY), f32),
            pltpu.VMEM((2, 2, CASES, NC, 2, NZ, NY), f32),
            pltpu.VMEM((NC, CASES, NX, NZ, NY), f32),
            pltpu.VMEM((CASES, 13, NX, NY), f32),
            pltpu.VMEM((CASES, 4, 8, NY), f32),
            pltpu.VMEM((2, NC, CASES, 8, NY), f32),
            pltpu.VMEM((2, NC, CASES, 8, NY), f32),
            pltpu.VMEM((2, NC, CASES, 8, NY), f32),
            pltpu.VMEM((NX + 4, CASES, NY), f32),
            pltpu.VMEM((CASES, NX, NY), f32),
            pltpu.VMEM((2, 4, 8, NY), f32),
            pltpu.VMEM((2, 2, 2, 8, NY), f32),
            pltpu.VMEM((2, 4, 8, NY), f32),
            pltpu.VMEM((2, 4, 8, NY), f32),
            pltpu.VMEM((1, 1, NY), f32),
            pltpu.VMEM((32, 1, NY), f32),
            pltpu.VMEM((1, 1, NY), f32),
            pltpu.VMEM((ZRING, 1, NY), f32),
            dma((4,)),
            dma((2,)),
            dma((NC,)),
            dma((2, 3, 2)),
            dma((2, 3, CASES, 2)),
            dma((2, 2)),
            dma((2, 2, CASES, 2)),
            dma((2,)),
            dma((2,)),
            dma((2, 2)),
            dma((2, 2)),
            dma((2,)),
            dma((2,)),
            pltpu.SemaphoreType.REGULAR,
        ],
        compiler_params=pltpu.CompilerParams(
            collective_id=0, has_side_effects=True, vmem_limit_bytes=48 * 1024 * 1024
        ),
        name="lubrication_adjoint",
    )(*given)


def solution(mesh):
    placed = (
        P(None, None, None, "roll", "trans"),
        P(None, None, None, "roll", "trans"),
        P(None, "roll", "trans"),
        P("roll", "trans"),
        P(None, "roll", "trans"),
        P(),
    )
    return jax.shard_map(
        on_device,
        mesh=mesh,
        in_specs=placed,
        out_specs=(P(None, None, None, "roll", "trans"), P("roll", "trans")),
        check_vma=False,
    )
```

```python
import jax
import jax.numpy as jnp
from jax import lax
from jax.experimental import pallas as pl
from jax.experimental.pallas import tpu as pltpu
from jax.sharding import PartitionSpec as P

VISCOSITY_PRESS = 0.3
VISCOSITY_TEMP = 0.5
THETA_STEP = 0.2
SOUND = 0.5
KAPPA = 0.6
HEATING = 0.3
COURANT = 0.8

MESH = pl.DeviceIdType.MESH
NC = 4
CASES = 2
NZ = 32
NX = 8
NY = 128
Z0 = 8
ZROWS = 48
ZT = NZ // 8
PIECES = 4
ZRING = 8
XGROUPS = (((0, 3), (3, 1)), ((0, 2), (2, 1), (3, 1)))
YGROUPS = (((0, 3), (3, 1)), ((0, 3), (3, 1)))

STEP, SLOPE, COUPLE, HEAT, A0, A1, A3, B0, B1, B3, C0, C1, C3 = range(13)
AROW = (A0, A1, A1, A3)
BROW = (B0, B1, B1, B3)
CROW = (C0, C1, C1, C3)


def kernel(
    adjoint, source, pressure_in, film_in, cavity_in, temp_in, out, wall,
    pressure, film, cavity, temp,
    s0, s1, halo, src, coef, pcoef, ysend, yleft, yright, mean, curv, zsum, zdiag, part, beside, mine, plane, mine2, ring,
    small_sem, in_sem, out_sem, xsend_sem, xrecv_sem, ysend_sem, yrecv_sem,
    msend_sem, mrecv_sem, dsend_sem, drecv_sem, rsend_sem, rrecv_sem, word,
):
    nr, nt = lax.axis_size("roll"), lax.axis_size("trans")
    r, t = lax.axis_index("roll"), lax.axis_index("trans")
    core = lax.rem(r, 2)
    z = lax.rem(r // 2, ZRING)
    g = r // (2 * ZRING)
    groups = nr // (2 * ZRING)
    plane_n = groups * 2 * nt
    cells = nr * NX * nt * NY

    def plane_peer(o):
        dt, dg, dc = o // (2 * groups), (o // 2) % groups, o % 2
        row = (lax.rem(g + dg, groups) * ZRING + z) * 2 + lax.rem(core + dc, 2)
        return (row, lax.rem(t + dt, nt))

    def ring_peer(o):
        return ((g * ZRING + lax.rem(z + o, ZRING)) * 2 + core, t)

    up = (lax.rem(r + 1, nr), t)
    down = (lax.rem(r + nr - 1, nr), t)
    right = (r, lax.rem(t + 1, nt))
    left = (r, lax.rem(t + nt - 1, nt))
    has_up, has_down = r < nr - 1, r > 0
    has_right, has_left = t < nt - 1, t > 0

    barrier = pltpu.get_barrier_semaphore()
    def hops(o):
        dt = o // (2 * groups)
        return min(dt % 4, 4 - dt % 4) + 2 * (dt >= 4) + (o // 2) % groups

    far_plane = sorted(range(1, plane_n), key=lambda o: -hops(o))
    far_ring = sorted(range(1, ZRING), key=lambda o: -min(o, ZRING - o))
    corners = [[(row[0], column[1]) for column in (right, left)] for row in (down, up)]
    y_phys = 2 * (t // 4) + g

    def in_plane(dx, dy, dc):
        y = lax.rem(y_phys + dy + 4, 4)
        row = ((lax.rem(y, 2)) * ZRING + z) * 2 + lax.rem(core + dc, 2)
        return (row, (y // 2) * 4 + lax.rem(lax.rem(t, 4) + dx + 4, 4))

    close = [
        in_plane(dx, dy, dc)
        for dx in (2, 1, -1, 0) for dy in (2, 1, -1, 0) for dc in (1, 0)
        if (dx, dy, dc) != (0, 0, 0) and abs(dx) + abs(dy) <= 2
    ]
    partners = [right, left, up, down] + [ring_peer(o) for o in (2, ZRING - 2, 1, ZRING - 1)] + close
    for peer in partners:
        pl.semaphore_signal(barrier, inc=1, device_id=peer, device_id_type=MESH)

    smalls = [
        pltpu.make_async_copy(given, held, small_sem.at[k])
        for k, (given, held) in enumerate(
            ((pressure_in, pressure), (film_in, film), (cavity_in, cavity), (temp_in, temp)))
    ]
    loads = [
        pltpu.make_async_copy(
            adjoint.at[:, :, :, x, :], s0.at[:, :, 2 + x, pl.ds(Z0, NZ), :], in_sem.at[0])
        for x in range(NX)
    ]
    src_loads = [
        pltpu.make_async_copy(source.at[:, :, :, x, :], src.at[:, :, x], in_sem.at[1])
        for x in range(NX)
    ]
    for copy in smalls + loads + src_loads:
        copy.start()

    lane = lax.broadcasted_iota(jnp.int32, (8, NY), 1)
    sub = lax.broadcasted_iota(jnp.int32, (8, NY), 0)
    lane4, lane_in4 = lane // 4, lane % 4
    lo_half = lane_in4 < 2
    near1, near2 = lane_in4 == 1, lane_in4 == 2
    rim = jnp.logical_or(lane < 2, lane >= NY - 2)
    heights = [(sub.astype(jnp.float32) + (8 * zt + 0.5)) / NZ for zt in range(ZT)]
    zero8 = jnp.zeros((8, NY), jnp.float32)

    for buf in (s0, s1):
        def clear(i, _, buf=buf):
            for case in range(CASES):
                for c in range(NC):
                    buf[c, case, i, 0:Z0, :] = zero8
                    buf[c, case, i, Z0 + NZ:ZROWS, :] = zero8
            return 0
        lax.fori_loop(0, NX + 4, clear, 0)

        def clear_row(i, _, buf=buf):
            for case in range(CASES):
                for x in (0, 1, NX + 2, NX + 3):
                    for zt in range(ZT):
                        buf[i, case, x, Z0 + 8 * zt:Z0 + 8 * zt + 8, :] = zero8
            return 0
        lax.fori_loop(0, NC, clear_row, 0)

    def clear_pack(i, _):
        for case in range(CASES):
            ysend[1, i, case] = zero8
        return 0
    lax.fori_loop(0, NC, clear_pack, 0)

    @pl.when(jnp.logical_not(has_down))
    def _():
        mean[0:2] = jnp.zeros((2, CASES, NY), jnp.float32)

    @pl.when(jnp.logical_not(has_up))
    def _():
        mean[NX + 2:NX + 4] = jnp.zeros((2, CASES, NY), jnp.float32)

    @pl.when(jnp.logical_not(has_left))
    def _():
        yleft[...] = jnp.zeros(yleft.shape, jnp.float32)
        zdiag[:, 0] = jnp.zeros((2, 2, 8, NY), jnp.float32)

    @pl.when(jnp.logical_not(has_right))
    def _():
        yright[...] = jnp.zeros(yright.shape, jnp.float32)
        zdiag[:, 1] = jnp.zeros((2, 2, 8, NY), jnp.float32)

    for copy in smalls:
        copy.wait()
    thick = film[...]
    for case in range(CASES):
        theta = THETA_STEP * temp[case].astype(jnp.float32)
        visc = jnp.exp(VISCOSITY_PRESS * pressure[case] - VISCOSITY_TEMP * theta)
        fcoef = 4.0 * visc / (thick * thick)
        density = 1.0 - 0.6 * cavity[case].astype(jnp.float32)
        step = COURANT / (32.0 / 3.0 * visc + 4.0 * fcoef + 2.0 * SOUND + 1.0)
        sv, sf = step * visc, step * fcoef
        table = {
            STEP: step, SLOPE: step * density / 12.0, COUPLE: step * (SOUND / 12.0), HEAT: HEATING * sv,
        }
        for scale, a, b, c in ((0.5, A0, B0, C0), (1.0, A1, B1, C1), (KAPPA, A3, B3, C3)):
            table[a] = (scale / 12.0) * sv
            table[b] = scale * sf
            table[c] = 1.0 - scale * (5.0 * sv + 2.0 * sf)
        for k, value in table.items():
            coef[case, k] = value
        for k, value in ((0, sv), (1, step)):
            acc = zero8
            for x in range(NX):
                here = jnp.logical_and(lane4 == ZT * x, sub == x)
                acc = jnp.where(here, pltpu.roll(value, 4 * ZT * x + 2, 1), acc)
            acc = acc + pltpu.roll(acc, 4, 1)
            acc = acc + pltpu.roll(acc, 8, 1)
            spread = jnp.broadcast_to(jnp.sum(acc, axis=0, keepdims=True), (8, NY))
            if k == 0:
                pcoef[case, 0] = (0.5 / 12.0) * spread
                pcoef[case, 1] = (1.0 / 12.0) * spread
                pcoef[case, 2] = (KAPPA / 12.0) * spread
            else:
                pcoef[case, 3] = (SOUND / 12.0) * spread

    for side in range(2):
        for k in range(4):
            zsum[side, k] = zero8
            part[side, k] = zero8
        for case in range(CASES):
            for i in range(2):
                x = (i, NX - 1 - i)[side]
                for j, k in enumerate((A0, SLOPE, COUPLE)):
                    part[side, 1 + j, 2 * case + i:2 * case + i + 1, :] = coef[case, k, x:x + 1, :]

    def x_copy(sec, grp, case, way):
        buf = (s0, s1)[sec]
        c, n = XGROUPS[sec][grp]
        a, peer = ((NX, up), (2, down))[way]
        return pltpu.make_async_remote_copy(
            src_ref=buf.at[pl.ds(c, n), case, pl.ds(a, 2), pl.ds(Z0, NZ), :],
            dst_ref=halo.at[sec, way, case, pl.ds(c, n)],
            send_sem=xsend_sem.at[sec, grp, way],
            recv_sem=xrecv_sem.at[sec, grp, case, way],
            device_id=peer, device_id_type=MESH)

    def y_copy(sec, grp, case, way):
        c, n = YGROUPS[sec][grp]
        dst, peer = ((yleft, right), (yright, left))[way]
        return pltpu.make_async_remote_copy(
            src_ref=ysend.at[sec, pl.ds(c, n), case],
            dst_ref=dst.at[sec, pl.ds(c, n), case],
            send_sem=ysend_sem.at[sec, way],
            recv_sem=yrecv_sem.at[sec, grp, case, way],
            device_id=peer, device_id_type=MESH)

    def x_start(sec, grp, case):
        for way, ok in ((0, has_up), (1, has_down)):
            @pl.when(ok)
            def _(way=way):
                x_copy(sec, grp, case, way).start()

    def y_start(sec, grp, case):
        for way, ok in ((0, has_right), (1, has_left)):
            @pl.when(ok)
            def _(way=way):
                y_copy(sec, grp, case, way).start()

    def y_wait(sec, grp, case):
        for way, ok in ((0, has_left), (1, has_right)):
            @pl.when(ok)
            def _(way=way):
                y_copy(sec, grp, case, way).wait_recv()

    def x_sent(sec, grp):
        c, n = XGROUPS[sec][grp]
        for way, ok in ((0, has_up), (1, has_down)):
            @pl.when(ok)
            def _(way=way):
                both = halo.at[sec, way, :, pl.ds(c, n)]
                pltpu.make_async_copy(both, both, xsend_sem.at[sec, grp, way]).wait()

    def y_sent(sec):
        for way, ok in ((0, has_right), (1, has_left)):
            @pl.when(ok)
            def _(way=way):
                pltpu.make_async_copy(ysend.at[sec], ysend.at[sec], ysend_sem.at[sec, way]).wait()

    def row_of(case, k, x):
        return jnp.broadcast_to(coef[case, k, pl.ds(x, 1), :], (8, NY))

    def packed(acc, tile, q):
        return jnp.where(lane4 == q, pltpu.roll(tile, 4 * q + 2, 1), acc)

    def inner(sec, case, comps, part_of=None):
        cur, new_buf = ((s0, s1), (s1, s0))[sec]
        need_x = sorted(set(comps) | ({1} if 0 in comps else set()) | ({0} if 1 in comps else set()))
        need_y = sorted(set(comps) | ({2} if 0 in comps else set()) | ({0} if 2 in comps else set()))

        def body(i, _):
            x = i + 4 * (i // 2) if part_of == 0 else i

            def row(k):
                return row_of(case, k, x)

            step, slope, couple = row(STEP), row(SLOPE), row(COUPLE)
            packs = {}
            if sec == 0:
                packs = {c: ysend[1, c, case] for c in comps}
            for zt in range(ZT):
                zs = Z0 + 8 * zt
                q = x * ZT + zt
                carry = slope * heights[zt]

                def at(c, dx=0, dz=0):
                    return cur[c, case, x + 2 + dx, zs + dz:zs + dz + 8, :]

                xd, yd, e1, e2 = {}, {}, {}, {}
                for c in need_y:
                    f = at(c)
                    p1, m1 = pltpu.roll(f, NY - 1, 1), pltpu.roll(f, 1, 1)
                    p2, m2 = pltpu.roll(f, NY - 2, 1), pltpu.roll(f, 2, 1)
                    if (c == 2 and 0 in comps) or (c == 0 and 2 in comps):
                        yd[c] = 8.0 * (p1 - m1) - (p2 - m2)
                    e1[c], e2[c] = p1 + m1, p2 + m2
                for c in need_x:
                    p1, m1, p2, m2 = at(c, 1), at(c, -1), at(c, 2), at(c, -2)
                    xd[c] = 8.0 * (p1 - m1) - (p2 - m2)
                    if c in comps:
                        e1[c], e2[c] = e1[c] + (p1 + m1), e2[c] + (p2 + m2)
                for c in comps:
                    new = row(CROW[c]) * at(c) + row(AROW[c]) * (16.0 * e1[c] - e2[c])
                    new = new + row(BROW[c]) * (at(c, 0, 1) + at(c, 0, -1))
                    new = new + (carry * xd[c] + step * src[c, case, x, 8 * zt:8 * zt + 8, :])
                    if c == 0:
                        new = new + couple * (xd[1] + yd[2])
                    elif c == 1:
                        new = new + couple * xd[0]
                    elif c == 2:
                        new = new + couple * yd[0]
                    else:
                        new = new + row(HEAT) * at(1)
                    new_buf[c, case, x + 2, zs:zs + 8, :] = new
                    if sec == 0:
                        packs[c] = packed(packs[c], new, q)
            for c, value in packs.items():
                ysend[1, c, case] = value
            return 0

        first, last = {None: (0, NX), 0: (0, 4), 1: (2, NX - 2)}[part_of]
        lax.fori_loop(first, last, body, 0, unroll=2)

    def rims(sec, case, comps):
        near, far, cross = {}, {}, {}
        for c in sorted(set(comps) | ({2} if 0 in comps else set()) | ({0} if 2 in comps else set())):
            d = jnp.where(lo_half, yleft[sec, c, case], yright[sec, c, case]) - ysend[sec, c, case]
            p1, m1 = pltpu.roll(d, NY - 1, 1), pltpu.roll(d, 1, 1)
            far_d = jnp.where(lo_half, pltpu.roll(d, NY - 2, 1), pltpu.roll(d, 2, 1))
            near[c] = 16.0 * jnp.where(near1, p1, jnp.where(near2, m1, 0.0)) - far_d
            cross[c] = 8.0 * jnp.where(near1, p1, jnp.where(near2, -m1, 0.0)) + jnp.where(lo_half, -far_d, far_d)
        result = {}
        for c in comps:
            value = pcoef[case, (0, 1, 1, 2)[c]] * near[c]
            if c in (0, 2):
                value = value + pcoef[case, 3] * cross[2 - c]
            result[c] = value
        return result

    def add_rims(sec, case, added, x):
        new_buf = (s1, s0)[sec]
        for c, value in added.items():
            for zt in range(ZT):
                zs = Z0 + 8 * zt
                here = jnp.where(rim, pltpu.roll(value, NY - 2 - 4 * (x * ZT + zt), 1), 0.0)
                new_buf[c, case, x + 2, zs:zs + 8, :] = new_buf[c, case, x + 2, zs:zs + 8, :] + here

    def edges(sec, grps, case, comps):
        new_buf = (s1, s0)[sec]
        added = rims(sec, case, comps)
        for x in (0, 1, NX - 2, NX - 1):
            add_rims(sec, case, added, x)
        if sec == 0:
            for c in comps:
                ysend[1, c, case] = ysend[1, c, case] + added[c]
        for way, ok in ((0, has_down), (1, has_up)):
            @pl.when(ok)
            def _(way=way):
                for grp in grps:
                    x_copy(sec, grp, case, way).wait_recv()
                packs = {c: zero8 for c in comps}
                outer, beside = ((0, 1), (NX - 1, NX - 2))[way]
                slopes = {x: row_of(case, SLOPE, x) for x in (outer, beside)}
                couples = {x: row_of(case, COUPLE, x) for x in (outer, beside)}
                for zt in range(ZT):
                    zs = Z0 + 8 * zt
                    h1, h2 = {}, {}
                    for c in sorted(set(comps) | ({1} if 0 in comps else set()) | ({0} if 1 in comps else set())):
                        first, second = ((1, 0), (0, 1))[way]
                        h1[c] = halo[sec, way, case, c, first, 8 * zt:8 * zt + 8, :]
                        h2[c] = halo[sec, way, case, c, second, 8 * zt:8 * zt + 8, :]
                    for x in (outer, beside):
                        carry = slopes[x] * heights[zt]
                        for c in comps:
                            mate = {0: 1, 1: 0}.get(c)
                            if x == outer:
                                lap = 16.0 * h1[c] - h2[c]
                                grad = lambda k: (h2[k] - 8.0 * h1[k]) if way == 0 else (8.0 * h1[k] - h2[k])
                            else:
                                lap = -h1[c]
                                grad = lambda k: h1[k] if way == 0 else -h1[k]
                            delta = row_of(case, AROW[c], x) * lap + carry * grad(c)
                            if mate is not None:
                                delta = delta + couples[x] * grad(mate)
                            new_buf[c, case, x + 2, zs:zs + 8, :] = new_buf[c, case, x + 2, zs:zs + 8, :] + delta
                            if sec == 0:
                                packs[c] = packed(packs[c], delta, x * ZT + zt)
                if sec == 0:
                    for c in comps:
                        ysend[1, c, case] = ysend[1, c, case] + packs[c]

    def middle(sec, case, comps):
        added = rims(sec, case, comps)

        def body(x, _):
            add_rims(sec, case, added, x)
            return 0

        lax.fori_loop(2, NX - 2, body, 0)

    pltpu.make_async_copy(adjoint, adjoint, in_sem.at[0]).wait()
    def pack_state(case, first, last):
        def pack_rows(x, accs):
            accs = list(accs)
            for c in range(first, last):
                for zt in range(ZT):
                    tile = s0[c, case, x + 2, Z0 + 8 * zt:Z0 + 8 * zt + 8, :]
                    accs[c - first] = packed(accs[c - first], tile, x * ZT + zt)
            return tuple(accs)

        accs = lax.fori_loop(0, NX, pack_rows, (zero8,) * (last - first), unroll=2)
        for c in range(first, last):
            ysend[0, c, case] = accs[c - first]

    for case in range(CASES):
        pack_state(case, 0, 3)
    pl.semaphore_wait(barrier, len(partners))
    for case in range(CASES):
        y_start(0, 0, case)
    for case in range(CASES):
        x_start(0, 0, case)
    for peer in partners:
        pl.semaphore_signal(word, inc=1, device_id=peer, device_id_type=MESH)
    pltpu.make_async_copy(source, source, in_sem.at[1]).wait()
    for case in range(CASES):
        inner(0, case, (0, 1, 2))
    for case in range(CASES):
        pack_state(case, 3, 4)
        inner(0, case, (3,))
    for case in range(CASES):
        y_wait(0, 0, case)
        edges(0, (0,), case, (0, 1, 2))
        y_start(1, 0, case)
        x_start(1, 0, case)
    for case in range(CASES):
        y_start(0, 1, case)
        x_start(0, 1, case)
        x_start(1, 1, case)

    pl.semaphore_wait(word, len(partners))

    def z_sum(buf, c, case, x, weights=None):
        total = None
        for zt in range(ZT):
            tile = buf[c, case, x + 2, Z0 + 8 * zt:Z0 + 8 * zt + 8, :]
            tile = tile if weights is None else tile * weights[zt]
            total = tile if total is None else total + tile
        return jnp.sum(total, axis=0, keepdims=True)

    for side in range(2):
        for case in range(CASES):
            for i in range(2):
                x = (i, NX - 1 - i)[side]
                at = slice(2 * case + i, 2 * case + i + 1)
                zsum[side, 0, at, :] = z_sum(s1, 0, case, x)
                zsum[side, 1, at, :] = z_sum(s1, 2, case, x)
                zsum[side, 2, at, :] = z_sum(s1, 1, case, x)
                zsum[side, 3, at, :] = z_sum(s1, 0, case, x, heights)

    has_row, has_column = (has_down, has_up), (has_right, has_left)

    def corner_copy(side, column):
        return pltpu.make_async_remote_copy(
            src_ref=zsum.at[side, pl.ds(0, 2)], dst_ref=zdiag.at[1 - side, column],
            send_sem=dsend_sem.at[side, column], recv_sem=drecv_sem.at[1 - side, column],
            device_id=corners[side][column], device_id_type=MESH)

    def corner_arrives(side, column):
        return pltpu.make_async_remote_copy(
            src_ref=zsum.at[side, pl.ds(0, 2)], dst_ref=zdiag.at[side, column],
            send_sem=dsend_sem.at[side, column], recv_sem=drecv_sem.at[side, column],
            device_id=corners[side][column], device_id_type=MESH)

    def part_copy(side, slot):
        return pltpu.make_async_remote_copy(
            src_ref=part.at[side], dst_ref=beside.at[slot],
            send_sem=msend_sem.at[side], recv_sem=mrecv_sem.at[slot],
            device_id=(down, up)[side], device_id_type=MESH)

    for side in range(2):
        for column in range(2):
            @pl.when(jnp.logical_and(has_row[side], has_column[column]))
            def _(side=side, column=column):
                corner_copy(side, column).start()

    for case in range(CASES):
        middle(0, case, (0, 1, 2))
    x_sent(0, 0)
    for case in range(CASES):
        inner(1, case, (0, 1), 0)

    def beyond(ghost):
        p1, m1 = pltpu.roll(ghost, NY - 1, 1), pltpu.roll(ghost, 1, 1)
        p2, m2 = pltpu.roll(ghost, NY - 2, 1), pltpu.roll(ghost, 2, 1)
        at0, at_end = lane == 0, lane == NY - 1
        lo, hi = lane < 2, lane >= NY - 2
        near = jnp.where(at_end, p1, jnp.where(at0, m1, 0.0))
        far = jnp.where(hi, p2, jnp.where(lo, m2, 0.0))
        near_x = jnp.where(at_end, p1, jnp.where(at0, -m1, 0.0))
        far_x = jnp.where(hi, p2, jnp.where(lo, -m2, 0.0))
        return 16.0 * near - far, 8.0 * near_x - far_x

    for side in range(2):
        for case in range(CASES):
            for i in range(2):
                x = (i, NX - 1 - i)[side]
                part[side, 0, 2 * case + i:2 * case + i + 1, :] = z_sum(s0, 0, case, x)
        ring_y, _unused = beyond(zsum[side, 0])
        _unused, ring_x = beyond(zsum[side, 1])
        part[side, 0] = part[side, 0] - part[side, 1] * ring_y - part[side, 3] * ring_x

        @pl.when(has_row[side])
        def _(side=side):
            part_copy(side, 1 - side).start()
    for case in range(CASES):
        inner(1, case, (0, 1), 1)

    for case in range(CASES):
        y_wait(1, 0, case)
        edges(1, (0,), case, (0, 1))
        middle(1, case, (0, 1))

        def rows_of(x, _, case=case):
            mean[x + 2, case:case + 1, :] = z_sum(s0, 0, case, x)
            bend = None
            for zt in range(ZT):
                zs = Z0 + 8 * zt
                f = s0[1, case, x + 2, zs:zs + 8, :]
                term = f * (s0[1, case, x + 2, zs + 1:zs + 9, :] - 2.0 * f + s0[1, case, x + 2, zs - 1:zs + 7, :])
                bend = term if bend is None else bend + term
            curv[case, pl.ds(x, 1), :] = jnp.sum(bend, axis=0, keepdims=True)
            return 0

        lax.fori_loop(0, NX, rows_of, 0, unroll=2)

    is_outer = sub % 2 == 0
    for slot in range(2):
        for column in range(2):
            @pl.when(jnp.logical_and(has_row[slot], (has_left, has_right)[column]))
            def _(slot=slot, column=column):
                corner_arrives(slot, column).wait_recv()

        @pl.when(has_row[slot])
        def _(slot=slot):
            part_copy(slot, slot).wait_recv()

            def lap(v, a):
                after, before = pltpu.roll(v, 7, 0), pltpu.roll(v, 1, 0)
                return jnp.where(is_outer, a * v - after, -before)

            sign = (1.0, -1.0)[slot]
            a0, slope, couple = beside[slot, 1], beside[slot, 2], beside[slot, 3]

            def ghost(k):
                return jnp.where(lane >= NY - 2, zdiag[slot, 0, k], jnp.where(lane < 2, zdiag[slot, 1, k], 0.0))

            lap_y, _unused = beyond(ghost(0))
            _unused, grad_y = beyond(ghost(1))
            value = beside[slot, 0] + a0 * (lap(zsum[slot, 0], 16.0) + lap_y)
            value = value + sign * (slope * lap(zsum[slot, 3], 8.0) + couple * lap(zsum[slot, 2], 8.0))
            value = value + couple * grad_y
            for case in range(CASES):
                for i in range(2):
                    row = (1 - i, NX + 2 + i)[slot]
                    mean[row, case:case + 1, :] = value[2 * case + i:2 * case + i + 1, :]

    def store_out(c):
        return [
            pltpu.make_async_copy(
                s0.at[c, :, 2 + x, pl.ds(Z0, NZ), :], out.at[c, :, :, x, :], out_sem.at[c])
            for x in range(NX)
        ]

    grad = jnp.zeros((NX, NY), jnp.float32)
    for case in range(CASES):
        theta = THETA_STEP * temp[case].astype(jnp.float32)
        visc = jnp.exp(VISCOSITY_PRESS * pressure[case] - VISCOSITY_TEMP * theta)
        density = 1.0 - 0.6 * cavity[case].astype(jnp.float32)

        def rows(dx):
            return mean[2 + dx:2 + dx + NX, case, :]

        slope = (8.0 * (rows(1) - rows(-1)) - (rows(2) - rows(-2))) / (12.0 * NZ)
        grad = grad + (density * thick / 2.0 * slope
                       - 8.0 * visc / (thick * thick * thick) * (curv[case] / NZ))
    wall[...] = grad
    mine[0] = jnp.sum(grad * grad, axis=0, keepdims=True)

    def plane_copy(o):
        return pltpu.make_async_remote_copy(
            src_ref=mine.at[0], dst_ref=plane.at[o], send_sem=rsend_sem.at[0], recv_sem=rrecv_sem.at[0],
            device_id=plane_peer(o), device_id_type=MESH)

    def ring_copy(o):
        return pltpu.make_async_remote_copy(
            src_ref=mine2.at[0], dst_ref=ring.at[o], send_sem=rsend_sem.at[1], recv_sem=rrecv_sem.at[1],
            device_id=ring_peer(o), device_id_type=MESH)

    for o in far_plane:
        plane_copy(o).start()

    for case in range(CASES):
        y_wait(0, 1, case)
        edges(0, (1,), case, (3,))
        y_start(1, 1, case)
        x_start(1, 2, case)
    for c in (0, 1):
        for copy in store_out(c):
            copy.start()
    for case in range(CASES):
        middle(0, case, (3,))
    x_sent(0, 1)
    for case in range(CASES):
        inner(1, case, (2, 3))
    pltpu.make_async_copy(plane.at[pl.ds(1, plane_n - 1)], plane.at[pl.ds(1, plane_n - 1)], rrecv_sem.at[0]).wait()
    mine2[0] = mine[0] + jnp.sum(plane[1:plane_n], axis=0)
    for o in far_ring:
        ring_copy(o).start()
    for case in range(CASES):
        y_wait(1, 1, case)
        edges(1, (1, 2), case, (2, 3))
        middle(1, case, (2, 3))
    for c in (2, 3):
        for copy in store_out(c):
            copy.start()
    pltpu.make_async_copy(plane.at[pl.ds(1, plane_n - 1)], plane.at[pl.ds(1, plane_n - 1)], rsend_sem.at[0]).wait()
    pltpu.make_async_copy(ring.at[pl.ds(1, ZRING - 1)], ring.at[pl.ds(1, ZRING - 1)], rsend_sem.at[1]).wait()
    for side in range(2):
        @pl.when(has_row[side])
        def _(side=side):
            part_copy(side, 1 - side).wait_send()
        for column in range(2):
            @pl.when(jnp.logical_and(has_row[side], has_column[column]))
            def _(side=side, column=column):
                corner_copy(side, column).wait_send()
    for grp in range(3):
        x_sent(1, grp)
    for sec in range(2):
        y_sent(sec)
    for c in range(NC):
        pltpu.make_async_copy(out.at[c], out.at[c], out_sem.at[c]).wait()

    pltpu.make_async_copy(ring.at[pl.ds(1, ZRING - 1)], ring.at[pl.ds(1, ZRING - 1)], rrecv_sem.at[1]).wait()
    total = jnp.sum(mine2[0] + jnp.sum(ring[1:ZRING], axis=0), axis=1, keepdims=True)
    wall[...] = wall[...] / jnp.sqrt(total / cells + 1e-06)


def store(state, wall, state_out, wall_out, sem):
    n = NC // PIECES
    copies = [pltpu.make_async_copy(wall, wall_out, sem.at[PIECES])] + [
        pltpu.make_async_copy(state.at[pl.ds(n * k, n)], state_out.at[pl.ds(n * k, n)], sem.at[k])
        for k in range(PIECES)
    ]
    for copy in copies:
        copy.start()
    for copy in copies:
        copy.wait()


def on_device(adjoint, source, pressure, film, cavity, temp_index):
    vmem = pl.BlockSpec(memory_space=pltpu.VMEM)
    hbm = pl.BlockSpec(memory_space=pltpu.HBM)
    f32 = jnp.float32
    dma = pltpu.SemaphoreType.DMA
    given = [
        pltpu.with_memory_space_constraint(a, pltpu.HBM)
        for a in (adjoint, source, pressure, film, cavity, temp_index)
    ]
    state, wall = pl.pallas_call(
        kernel,
        out_shape=(pltpu.VMEM(adjoint.shape, f32), pltpu.VMEM(film.shape, f32)),
        in_specs=[hbm] * 6,
        out_specs=(vmem, vmem),
        scratch_shapes=[
            pltpu.VMEM(pressure.shape, f32),
            pltpu.VMEM(film.shape, f32),
            pltpu.VMEM(cavity.shape, jnp.int32),
            pltpu.SMEM(temp_index.shape, jnp.int32),
            pltpu.VMEM((NC, CASES, NX + 4, ZROWS, NY), f32),
            pltpu.VMEM((NC, CASES, NX + 4, ZROWS, NY), f32),
            pltpu.VMEM((2, 2, CASES, NC, 2, NZ, NY), f32),
            pltpu.VMEM((NC, CASES, NX, NZ, NY), f32),
            pltpu.VMEM((CASES, 13, NX, NY), f32),
            pltpu.VMEM((CASES, 4, 8, NY), f32),
            pltpu.VMEM((2, NC, CASES, 8, NY), f32),
            pltpu.VMEM((2, NC, CASES, 8, NY), f32),
            pltpu.VMEM((2, NC, CASES, 8, NY), f32),
            pltpu.VMEM((NX + 4, CASES, NY), f32),
            pltpu.VMEM((CASES, NX, NY), f32),
            pltpu.VMEM((2, 4, 8, NY), f32),
            pltpu.VMEM((2, 2, 2, 8, NY), f32),
            pltpu.VMEM((2, 4, 8, NY), f32),
            pltpu.VMEM((2, 4, 8, NY), f32),
            pltpu.VMEM((1, 1, NY), f32),
            pltpu.VMEM((32, 1, NY), f32),
            pltpu.VMEM((1, 1, NY), f32),
            pltpu.VMEM((ZRING, 1, NY), f32),
            dma((4,)),
            dma((2,)),
            dma((NC,)),
            dma((2, 3, 2)),
            dma((2, 3, CASES, 2)),
            dma((2, 2)),
            dma((2, 2, CASES, 2)),
            dma((2,)),
            dma((2,)),
            dma((2, 2)),
            dma((2, 2)),
            dma((2,)),
            dma((2,)),
            pltpu.SemaphoreType.REGULAR,
        ],
        compiler_params=pltpu.CompilerParams(
            collective_id=0, has_side_effects=True, vmem_limit_bytes=48 * 1024 * 1024
        ),
        name="lubrication_adjoint",
    )(*given)
    return pl.pallas_call(
        store,
        out_shape=(pltpu.HBM(adjoint.shape, f32), pltpu.HBM(film.shape, f32)),
        in_specs=[vmem, vmem],
        out_specs=(hbm, hbm),
        scratch_shapes=[dma((PIECES + 1,))],
        name="store",
    )(*[pltpu.with_memory_space_constraint(a, pltpu.VMEM) for a in (state, wall)])


def solution(mesh):
    placed = (
        P(None, None, None, "roll", "trans"),
        P(None, None, None, "roll", "trans"),
        P(None, "roll", "trans"),
        P("roll", "trans"),
        P(None, "roll", "trans"),
        P(),
    )
    return jax.shard_map(
        on_device,
        mesh=mesh,
        in_specs=placed,
        out_specs=(P(None, None, None, "roll", "trans"), P("roll", "trans")),
        check_vma=False,
    )
```
